32 devices in a mesh: groups: 2 (over y), uv: 4 (over z), pol: 2 (over x), sub: 2 (over core).
Axes of the slice: x: 2, y: 2, z: 4, core: 2. Of those that a mesh axis runs over, the one named last changes fastest.
Arguments:
- visibilities: bfloat16 [2, 512, 256, 512], P(None, 'uv', 'groups', ('pol', 'sub')), parts along dimension 2, may hold values from -6 to 6
- flags: int32 [1024], P(('groups', 'uv')), parts along dimension 0, may hold values 0 or 1
- delays: int32 [512, 512], replicated, may hold values from 0 to 1023, as said below
- coord_u: int32 [512], replicated, may hold values from 0 to 127
- coord_v: int32 [512], replicated, may hold values from 0 to 63
Outputs:
- images: float32 [1024, 128, 128], P(('groups', 'uv', 'pol', 'sub')), parts along dimension 0
- snr: float32 [1024], P(('groups', 'uv', 'pol', 'sub')), parts along dimension 0
The draws below stay inside these ranges and needn't reach their ends.
There are 2 independent parts, one for each index of `groups`. The reference program is written for one: setup_inputs(seed, part) draws one part's arguments, and reference() takes and returns one part's arrays. A program takes and returns all parts, laid end to end along the dimension named above; an argument that names none is the same for every part. Nothing has to cross between parts.
Inputs may be any that keep to these rules, and one draw needn't show every extreme that they name: delays grow with the DM trial and fall with the channel index, with a small irregular part and a common offset, taken modulo 8 * 128.
All inputs are finite; a program needn't handle non-finite values. No bound on the sum of `flags` on one device may be relied on, other than what follows from the above.
Results may differ from the reference program's by a relative error of at most 0.0003.
Values sent between devices are 32-bit elements; how exact they have to be, the bound alone decides.
No kernel may reach another device: no remote copies, remote signals or barrier semaphores. Data moves between devices by JAX's collectives and lax.ppermute only.
A program may use at most 64 MiB of HBM per device.

```python
import math
import jax
import jax.numpy as jnp
from jax import lax

C = 512
NT = 128
D = 512
IMG = 128
FRAC = 8
NV = 512


def draw_delays(key, part):
    base = jax.random.fold_in(key, 11)
    first, second, third = jax.random.split(base, 3)
    trial_steps = jax.random.randint(first, (D,), 0, 3)
    measure = jnp.cumsum(trial_steps)
    channel_steps = jax.random.randint(second, (C,), 0, 5)
    curve = jnp.cumsum(channel_steps[::-1])[::-1]
    jitter = jax.random.randint(third, (D, C), 0, 8)
    cycle = FRAC * NT
    raw = (measure[:, None] * curve[None, :] // 16 + jitter) % cycle
    offset = cycle - 1 - raw[D - 1, 0]
    return (raw + offset) % cycle


def place_ends(drawn, own_key, smallest, high):
    extent = drawn.shape
    index_at = [jax.random.randint(jax.random.fold_in(own_key, axis), (), 0, extent[axis]) for axis in range(len(extent))]
    drawn = drawn.at[tuple(index_at)].set(smallest)
    longest = extent.index(max(extent))
    index_at[longest] = (index_at[longest] + 1) % extent[longest]
    return drawn.at[tuple(index_at)].set(high)


def steps_of(key, dims, shards, low, high):
    level, own = 1.0, jax.random.fold_in(key, 6)
    for dim, blocks in shards:
        steps = jnp.exp(jax.random.uniform(jax.random.fold_in(own, dim), (blocks,), jnp.float32, low / len(shards), high / len(shards)))
        level = level * jnp.repeat(steps, dims[dim] // blocks).reshape([-1 if axis == dim else 1 for axis in range(len(dims))])
    return level


def centred(own_key, dims, scale, most, cuts=(), held_as=jnp.bfloat16):
    array = scale * jax.random.normal(own_key, dims, jnp.float32)
    if cuts:
        array = array * steps_of(own_key, dims, cuts, -0.22, 0.18)
    return jnp.clip(array, -most, most).astype(held_as)


def setup_inputs(seed: int = 0, part: int = 0) -> dict:
    streams_of = jax.random.split(jax.random.key(seed), 6)
    own_keys = jax.random.split(jax.random.fold_in(streams_of[5], part), 6)
    visibilities = centred(own_keys[0], (2, C, NT, NV), 1.0, 6.0, ((1, 4), (3, 4)))
    flags = place_ends((jax.random.randint(own_keys[1], (C,), 0, 4) < 3).astype(jnp.int32), jax.random.fold_in(own_keys[1], 1), 0, 1)
    delays = draw_delays(jax.random.fold_in(streams_of[5], 71), part)
    coord_u = place_ends(jax.random.randint(streams_of[3], (NV,), 0, IMG), jax.random.fold_in(streams_of[3], 1), 0, IMG - 1).astype(jnp.int32)
    coord_v = place_ends(jax.random.randint(streams_of[4], (NV,), 0, IMG // 2), jax.random.fold_in(streams_of[4], 1), 0, (IMG // 2) - 1).astype(jnp.int32)
    return dict(visibilities=visibilities, flags=flags, delays=delays, coord_u=coord_u, coord_v=coord_v)


def twiddle(length):
    steps = jnp.arange(length, dtype=jnp.int32)
    angle = (steps[:, None] * steps[None, :] % length).astype(jnp.float32) * (2.0 * math.pi / length)
    return (jnp.cos(angle), jnp.sin(angle))

def spectrum(samples):
    cosine, sine = twiddle(samples.shape[2])
    precise = lax.Precision.HIGHEST
    spectrum_real = jnp.einsum('ft,ctk->cfk', cosine, samples[0], precision=precise) + jnp.einsum('ft,ctk->cfk', sine, samples[1], precision=precise)
    spectrum_imag = jnp.einsum('ft,ctk->cfk', cosine, samples[1], precision=precise) - jnp.einsum('ft,ctk->cfk', sine, samples[0], precision=precise)
    return (spectrum_real, spectrum_imag)

def signed_frequencies(length):
    steps = jnp.arange(length, dtype=jnp.int32)
    return jnp.where(steps >= length // 2, steps - length, steps)

def rotation(delay_rows, frequencies, cycle):
    index = delay_rows[:, :, None] * frequencies[None, None, :] % cycle
    angle = index.astype(jnp.float32) * (2.0 * math.pi / cycle)
    angle = angle.reshape(delay_rows.shape[0], delay_rows.shape[1] * frequencies.shape[0])
    return (jnp.cos(angle), jnp.sin(angle))

def picture(sum_real, sum_imag, coord_u, coord_v, side, weight):
    precise = lax.Precision.HIGHEST
    pixels = jnp.arange(side, dtype=jnp.int32)
    row_angle = (pixels[:, None] * coord_u[None, :] % side).astype(jnp.float32) * (2.0 * math.pi / side)
    column_angle = (coord_v[:, None] * pixels[None, :] % side).astype(jnp.float32) * (2.0 * math.pi / side)
    row_cosine, row_sine = (jnp.cos(row_angle), jnp.sin(row_angle))
    first = sum_real[:, None, :] * row_cosine[None] - sum_imag[:, None, :] * row_sine[None]
    second = sum_real[:, None, :] * row_sine[None] + sum_imag[:, None, :] * row_cosine[None]
    image = jnp.einsum('dlk,km->dlm', first, jnp.cos(column_angle), precision=precise) - jnp.einsum('dlk,km->dlm', second, jnp.sin(column_angle), precision=precise)
    return image * weight

def reference(visibilities, flags, delays, coord_u, coord_v):
    precise = lax.Precision.HIGHEST
    samples = visibilities.astype(jnp.float32)
    spectrum_real, spectrum_imag = spectrum(samples)
    keep = flags.astype(jnp.float32)[:, None, None]
    spectrum_real = spectrum_real * keep
    spectrum_imag = spectrum_imag * keep
    frequencies = signed_frequencies(NT)

    def accumulate(index, totals):
        where_at = jnp.asarray(index).astype(jnp.int32)
        cosine, sine = rotation(delays, lax.dynamic_slice_in_dim(frequencies, where_at, 1), FRAC * NT)
        column_real = lax.dynamic_index_in_dim(spectrum_real, where_at, 1, keepdims=False)
        column_imag = lax.dynamic_index_in_dim(spectrum_imag, where_at, 1, keepdims=False)
        total_real = totals[0] + jnp.dot(cosine, column_real, precision=precise) - jnp.dot(sine, column_imag, precision=precise)
        total_imag = totals[1] + jnp.dot(sine, column_real, precision=precise) + jnp.dot(cosine, column_imag, precision=precise)
        return (total_real, total_imag)
    begin = (jnp.zeros((D, NV), jnp.float32), jnp.zeros((D, NV), jnp.float32))
    sum_real, sum_imag = lax.fori_loop(0, NT, accumulate, begin)
    scale = 1.0 / math.sqrt(C * NT)
    sum_real = sum_real * scale
    sum_imag = sum_imag * scale
    weight = 2.0 / math.sqrt(NV)

    def one_trial(pair):
        return picture(pair[0][None], pair[1][None], coord_u, coord_v, IMG, weight)[0]
    images = lax.map(one_trial, (sum_real, sum_imag))
    peaks = lax.optimization_barrier(jnp.max(images, axis=(1, 2)))
    power = lax.optimization_barrier(jnp.mean(images * images, axis=(1, 2)))
    snr = peaks / jnp.sqrt(power + 1e-06)
    return (images, snr)
```

```python
import functools
import math

import jax
import jax.numpy as jnp
import numpy as np
from jax import lax
from jax.experimental import pallas as pl
from jax.experimental.pallas import tpu as pltpu
from jax.sharding import PartitionSpec as P

IMG = 128
FRAC = 8
AXES = ("uv", "pol", "sub")
F32 = jnp.float32
BF16 = jnp.bfloat16


def time_tables(times):
    t = np.arange(times)
    cot = np.where(t == 0, 2.0**60, 1.0 / np.tan(np.pi * np.where(t == 0, 1, t) / times))
    cot[times // 2] = 0.0
    cot = cot.astype(np.float32).astype(np.float64)
    power = 2.0 ** np.floor(16 - np.log2(np.maximum(np.abs(cot), 2.0**-10)))
    shifted = cot * power - np.where(t % 2 == 0, 1.0, -1.0) / times
    folded = np.minimum(t, times // 2)
    rows = [np.sin(np.pi * folded / times), np.cos(np.pi * folded / times), power, shifted]
    table = np.repeat(np.stack(rows), 8, axis=0).astype(np.float32)
    column = np.repeat(cot[:, None], 128, axis=1).astype(np.float32)
    return table, column


def coefficients(n, table, times):
    cycle = FRAC * times
    lanes = table.shape[1]
    parts = [[], [], [], []]
    for j in range(n.shape[1] // lanes):
        part = n[:, j * lanes : (j + 1) * lanes]
        fold = jnp.minimum(part, cycle - part)
        for i in range(4):
            index = (fold if i < 2 else part) >> 3
            parts[i].append(jnp.take_along_axis(table[i * 8 : (i + 1) * 8], index, axis=1))
    sin_q, cos_q, power, shifted = [jnp.concatenate(p, axis=1) for p in parts]
    fold = jnp.minimum(n, cycle - n)
    theta = (fold & (FRAC - 1)).astype(F32) * (math.pi / cycle)
    square = theta * theta
    cos_r = 1.0 - square * (0.5 - square * (1.0 / 24.0))
    sin_r = theta * (1.0 - square * (1.0 / 6.0 - square * (1.0 / 120.0)))
    sin_a = sin_q * cos_r + cos_q * sin_r
    cos_a = cos_q * cos_r - sin_q * sin_r
    cos_a = jnp.where(n + n > cycle, -cos_a, cos_a)
    r = n & (FRAC - 1)
    side = jnp.abs(r - FRAC // 2)
    size = [math.cos(math.pi * i / FRAC) for i in range(FRAC // 2)]
    s = jnp.where(side == 0, size[0], jnp.where(side == 1, size[1], jnp.where(side == 2, size[2], size[3])))
    s = jnp.where((n & FRAC) == 0, s, -s)
    whole = r == 0
    ratio = sin_a / s
    u = jnp.where(whole, power, sin_a * ratio)
    w = jnp.where(whole, shifted, cos_a * ratio)
    k = jnp.where(whole, 0.0, s * cos_a / jnp.where(whole, 1.0, sin_a))
    return u, w, k, jnp.where(whole, 0.0, s)


def dedisperse_kernel(
    flags_ref, delays_ref, table_ref, column_ref, sign_ref, vis_hbm, out_ref,
    vis_ref, sem, acc_ref, u_ref, w_ref, k_ref, sums_ref, *pairs,
    channels, times, cells, block, group, copies, scale,
):
    trials = delays_ref.shape[2]
    per = channels // copies

    def copy(i, p):
        rows = pl.ds(i * per, per)
        return pltpu.make_async_copy(vis_hbm.at[p, rows], vis_ref.at[p, rows], sem.at[p, i])

    for i in range(copies):
        for p in range(2):
            copy(i, p).start()
    table = table_ref[...]

    def prepare(i, carry):
        u, w, k, s = coefficients(delays_ref[i], table, times)
        u_ref[i] = u
        w_ref[i] = w
        rows = pl.ds(pl.multiple_of(i * 8, 8), 8)
        k_ref[rows, :] = k
        k_ref[pl.ds(pl.multiple_of(channels + i * 8, 8), 8), :] = s
        return carry

    lax.fori_loop(0, channels // 8, prepare, 0)
    acc_ref[...] = jnp.zeros_like(acc_ref)
    sign_rows = sign_ref[...]
    column_sign = jnp.where(lax.broadcasted_iota(jnp.int32, (8, cells), 0) % 2 == 0, 1.0, -1.0)

    def body(step, carry):
        total = None
        for i in range(block // group):
            right, left = pairs[2 * i], pairs[2 * i + 1]
            for j in range(group):
                at = i * group + j
                c = step * block + at
                keep = flags_ref[c].astype(F32)
                signs = (sign_rows * keep).astype(BF16)
                for p in range(2):
                    sample = vis_ref[p, c]
                    left[p * cells : (p + 1) * cells, j * times : (j + 1) * times] = sample.T * signs
                    wide = sample.astype(F32)
                    part = wide[0:8]
                    for t in range(8, times, 8):
                        part = part + wide[t : t + 8]
                    row = jnp.sum(part * column_sign, axis=0, keepdims=True) * keep
                    sums_ref[step * (block // 8) + at // 8, at % 8 : at % 8 + 1, p * cells : (p + 1) * cells] = row
                for b in range(0, trials, 128):
                    row = step * (block // 8) + at // 8
                    u = u_ref[row, at % 8 : at % 8 + 1, b : b + 128]
                    w = w_ref[row, at % 8 : at % 8 + 1, b : b + 128]
                    for t in range(0, times, 16):
                        bottom = column_ref[t : t + 16, :] * u - w
                        guess = pltpu.reciprocal(bottom, approx=True)
                        high = guess.astype(BF16)
                        rest = (1.0 - bottom * high.astype(F32)) * guess
                        rows = slice(j * times + t, j * times + t + 16)
                        right[rows, b : b + 128] = high
                        right[rows, trials + b : trials + b + 128] = rest.astype(BF16)
            one = jnp.dot(left[...], right[...], preferred_element_type=F32)
            total = one if total is None else total + one
        acc_ref[...] += total
        return carry

    steps = channels // block // copies
    for i in range(copies):
        for p in range(2):
            copy(i, p).wait()
        lax.fori_loop(i * steps, (i + 1) * steps, body, 0)

    sums = sums_ref[...].reshape(channels, 2 * cells)
    real, imag = sums[:, :cells], sums[:, cells:]
    lower = jnp.concatenate([imag, -real], axis=1)
    right = jnp.concatenate([sums, lower], axis=0)
    extra = jnp.dot(k_ref[...].T, right, precision=lax.Precision.HIGHEST, preferred_element_type=F32)
    main = (acc_ref[:, :trials] + acc_ref[:, trials:]).T
    out_ref[...] = (main + extra) * scale


def dedisperse(flags, delays, visibilities, scale):
    _, channels, times, cells = visibilities.shape
    trials = delays.shape[2]
    table, column = time_tables(times)
    sign = np.where(np.arange(times) % 2 == 0, 1.0, -1.0).astype(np.float32)[None, :]
    block = min(16, channels)
    group = 2
    copies = min(4, channels // block)
    vmem = pl.BlockSpec(memory_space=pltpu.VMEM)
    scratch = [
        pltpu.VMEM(visibilities.shape, visibilities.dtype),
        pltpu.SemaphoreType.DMA((2, copies)),
        pltpu.VMEM((2 * cells, 2 * trials), F32),
        pltpu.VMEM((channels // 8, 8, trials), F32),
        pltpu.VMEM((channels // 8, 8, trials), F32),
        pltpu.VMEM((2 * channels, trials), F32),
        pltpu.VMEM((channels // 8, 8, 2 * cells), F32),
    ]
    for _ in range(block // group):
        scratch += [pltpu.VMEM((group * times, 2 * trials), BF16), pltpu.VMEM((2 * cells, group * times), BF16)]
    return pl.pallas_call(
        functools.partial(
            dedisperse_kernel, channels=channels, times=times, cells=cells,
            block=block, group=group, copies=copies, scale=scale,
        ),
        in_specs=[pl.BlockSpec(memory_space=pltpu.SMEM), vmem, vmem, vmem, vmem, pl.BlockSpec(memory_space=pl.ANY)],
        out_specs=vmem,
        out_shape=jax.ShapeDtypeStruct((trials, 2 * cells), F32),
        scratch_shapes=scratch,
        compiler_params=pltpu.CompilerParams(vmem_limit_bytes=60 << 20),
        name="dedisperse",
    )(flags, delays, jnp.asarray(table), jnp.asarray(column), jnp.asarray(sign), visibilities)


def image_kernel(sums_ref, cos_ref, sin_ref, right_ref, image_ref, snr_ref, real_ref, imag_ref, peak_ref, power_ref, *, side, weight):
    blocks = sums_ref.shape[1]
    trials = sums_ref.shape[2]
    cells = sums_ref.shape[3] // 2
    for b in range(blocks):
        total = sums_ref[0, b]
        for i in range(1, sums_ref.shape[0]):
            total = total + sums_ref[i, b]
        total = total * weight
        real_ref[:, b * cells : (b + 1) * cells] = total[:, :cells]
        imag_ref[:, b * cells : (b + 1) * cells] = total[:, cells:]
    right = right_ref[...]
    for d in range(trials):
        real = real_ref[d : d + 1, :]
        imag = imag_ref[d : d + 1, :]
        cosine, sine = cos_ref[...], sin_ref[...]
        first = real * cosine - imag * sine
        second = -(real * sine + imag * cosine)
        left = jnp.concatenate([first, second], axis=1)
        high = left.astype(BF16)
        low = (left - high.astype(F32)).astype(BF16)
        one = jnp.dot(jnp.concatenate([high, low], axis=0), right, preferred_element_type=F32)
        image = one[:side, :side] + (one[:side, side:] + one[side:, :side])
        image_ref[d] = image
        peak_ref[d : d + 1, :] = jnp.max(image, axis=0, keepdims=True)
        power_ref[d : d + 1, :] = jnp.sum(image * image, axis=0, keepdims=True)
    peak = jnp.max(peak_ref[...], axis=1, keepdims=True)
    power = jnp.sum(power_ref[...], axis=1, keepdims=True) / (side * side)
    snr_ref[...] = peak / jnp.sqrt(power + 1e-06)


def picture(sums, coord_u, coord_v, side, weight):
    total = coord_u.shape[0]
    trials = sums.shape[2]
    pixels = jnp.arange(side, dtype=jnp.int32)
    row_angle = (pixels[:, None] * coord_u[None, :] % side).astype(F32) * (2.0 * math.pi / side)
    column_angle = (coord_v[:, None] * pixels[None, :] % side).astype(F32) * (2.0 * math.pi / side)
    columns = jnp.concatenate([jnp.cos(column_angle), jnp.sin(column_angle)], axis=0)
    high = lax.reduce_precision(columns, 8, 7)
    right = jnp.concatenate([high.astype(BF16), (columns - high).astype(BF16)], axis=1)
    vmem = pl.BlockSpec(memory_space=pltpu.VMEM)
    images, snr = pl.pallas_call(
        functools.partial(image_kernel, side=side, weight=weight),
        in_specs=[vmem] * 4,
        out_specs=[vmem] * 2,
        out_shape=[jax.ShapeDtypeStruct((trials, side, side), F32), jax.ShapeDtypeStruct((trials, 1), F32)],
        scratch_shapes=[pltpu.VMEM((trials, total), F32)] * 2 + [pltpu.VMEM((trials, side), F32)] * 2,
        compiler_params=pltpu.CompilerParams(vmem_limit_bytes=60 << 20),
        name="picture",
    )(sums, jnp.cos(row_angle), jnp.sin(row_angle), right)
    return images, snr[:, 0]


def shards(visibilities, flags, delays, coord_u, coord_v, *, sizes):
    channels = visibilities.shape[1]
    times = visibilities.shape[2]
    cells = visibilities.shape[3]
    trials, total_channels = delays.shape
    position = lax.axis_index("uv")
    rows = lax.dynamic_slice_in_dim(delays, position * channels, channels, 1).T
    scale = 1.0 / math.sqrt(total_channels * times)
    part = dedisperse(flags, rows.reshape(channels // 8, 8, trials), visibilities, scale)
    owners = sizes["uv"] * sizes["pol"] * sizes["sub"]
    held = lax.all_to_all(part.reshape(owners, trials // owners, 2 * cells), AXES, split_axis=0, concat_axis=0, tiled=True)
    held = held.reshape(sizes["uv"], sizes["pol"] * sizes["sub"], trials // owners, 2 * cells)
    weight = 2.0 / math.sqrt(coord_u.shape[0])
    return picture(held, coord_u, coord_v, IMG, weight)


def solution(mesh):
    in_specs = (P(None, "uv", "groups", ("pol", "sub")), P(("groups", "uv")), P(), P(), P())
    out_specs = (P(("groups", "uv", "pol", "sub"), None, None), P(("groups", "uv", "pol", "sub")))
    body = functools.partial(shards, sizes=dict(mesh.shape))
    return jax.shard_map(body, mesh=mesh, in_specs=in_specs, out_specs=out_specs, check_vma=False)
```

```python
import functools
import math

import jax
import jax.numpy as jnp
import numpy as np
from jax import lax
from jax.experimental import pallas as pl
from jax.experimental.pallas import tpu as pltpu
from jax.sharding import PartitionSpec as P

IMG = 128
FRAC = 8
AXES = ("uv", "pol", "sub")
F32 = jnp.float32
BF16 = jnp.bfloat16


def time_tables(times):
    t = np.arange(times)
    cot = np.where(t == 0, 2.0**60, 1.0 / np.tan(np.pi * np.where(t == 0, 1, t) / times))
    cot[times // 2] = 0.0
    cot = cot.astype(np.float32).astype(np.float64)
    power = 2.0 ** np.floor(16 - np.log2(np.maximum(np.abs(cot), 2.0**-10)))
    shifted = cot * power - np.where(t % 2 == 0, 1.0, -1.0) / times
    folded = np.minimum(t, times // 2)
    rows = [np.sin(np.pi * folded / times), np.cos(np.pi * folded / times), power, shifted]
    table = np.repeat(np.stack(rows), 8, axis=0).astype(np.float32)
    column = np.repeat(cot[:, None], 128, axis=1).astype(np.float32)
    return table, column


def coefficients(n, table, times):
    cycle = FRAC * times
    lanes = table.shape[1]
    parts = [[], [], [], []]
    for j in range(n.shape[1] // lanes):
        part = n[:, j * lanes : (j + 1) * lanes]
        fold = jnp.minimum(part, cycle - part)
        for i in range(4):
            index = (fold if i < 2 else part) >> 3
            parts[i].append(jnp.take_along_axis(table[i * 8 : (i + 1) * 8], index, axis=1))
    sin_q, cos_q, power, shifted = [jnp.concatenate(p, axis=1) for p in parts]
    fold = jnp.minimum(n, cycle - n)
    theta = (fold & (FRAC - 1)).astype(F32) * (math.pi / cycle)
    square = theta * theta
    cos_r = 1.0 - square * (0.5 - square * (1.0 / 24.0))
    sin_r = theta * (1.0 - square * (1.0 / 6.0 - square * (1.0 / 120.0)))
    sin_a = sin_q * cos_r + cos_q * sin_r
    cos_a = cos_q * cos_r - sin_q * sin_r
    cos_a = jnp.where(n + n > cycle, -cos_a, cos_a)
    r = n & (FRAC - 1)
    side = jnp.abs(r - FRAC // 2)
    size = [math.cos(math.pi * i / FRAC) for i in range(FRAC // 2)]
    s = jnp.where(side == 0, size[0], jnp.where(side == 1, size[1], jnp.where(side == 2, size[2], size[3])))
    s = jnp.where((n & FRAC) == 0, s, -s)
    whole = r == 0
    ratio = sin_a / s
    u = jnp.where(whole, power, sin_a * ratio)
    w = jnp.where(whole, shifted, cos_a * ratio)
    k = jnp.where(whole, 0.0, s * cos_a / jnp.where(whole, 1.0, sin_a))
    return u, w, k, jnp.where(whole, 0.0, s)


def prepare(delays_ref, table_ref, u_ref, w_ref, k_ref, channels, times):
    table = table_ref[...]

    def body(i, carry):
        u, w, k, s = coefficients(delays_ref[i], table, times)
        u_ref[i] = u
        w_ref[i] = w
        k_ref[pl.ds(pl.multiple_of(i * 8, 8), 8), :] = k
        k_ref[pl.ds(pl.multiple_of(channels + i * 8, 8), 8), :] = s
        return carry

    lax.fori_loop(0, channels // 8, body, 0)


def fill(right, u, w, column_ref, start, times):
    tiles = len(right) // 2
    for b in range(tiles):
        lanes = slice(b * 128, (b + 1) * 128)
        for t in range(0, times, 16):
            bottom = column_ref[t : t + 16, :] * u[:, lanes] - w[:, lanes]
            guess = pltpu.reciprocal(bottom, approx=True)
            high = guess.astype(BF16)
            rest = (1.0 - bottom * high.astype(F32)) * guess
            right[b][start + t : start + t + 16, :] = high
            right[tiles + b][start + t : start + t + 16, :] = rest.astype(BF16)


def join(refs):
    return jnp.concatenate([ref[...] for ref in refs], axis=1)


def finish(acc_ref, k_ref, sums, out_ref, trials, scale):
    cells = sums.shape[1] // 2
    real, imag = sums[:, :cells], sums[:, cells:]
    right = jnp.concatenate([sums, jnp.concatenate([imag, -real], axis=1)], axis=0)
    extra = jnp.dot(k_ref[...].T, right, precision=lax.Precision.HIGHEST, preferred_element_type=F32)
    main = (acc_ref[:, :trials] + acc_ref[:, trials:]).T
    out_ref[...] = (main + extra) * scale


def first_kernel(
    flags_ref, delays_ref, table_ref, column_ref, sign_ref, vis_ref, out_ref, turned_ref, sums_ref,
    acc_ref, u_ref, w_ref, k_ref, *pairs, block, group, scale,
):
    _, channels, times, cells = vis_ref.shape
    trials = delays_ref.shape[2]
    tiles = 2 * (trials // 128)
    prepare(delays_ref, table_ref, u_ref, w_ref, k_ref, channels, times)
    acc_ref[...] = jnp.zeros_like(acc_ref)
    sign_rows = sign_ref[...]
    column_sign = jnp.where(lax.broadcasted_iota(jnp.int32, (8, cells), 0) % 2 == 0, 1.0, -1.0)

    def body(step, carry):
        total = None
        for i in range(block // group):
            at = i * (tiles + group)
            right, left = pairs[at : at + tiles], pairs[at + tiles : at + tiles + group]
            for j in range(group):
                at = i * group + j
                c = step * block + at
                row = step * (block // 8) + at // 8
                one = slice(at % 8, at % 8 + 1)
                keep = flags_ref[c].astype(F32)
                signs = (sign_rows * keep).astype(BF16)
                for p in range(2):
                    sample = vis_ref[p, c]
                    turned = sample.T * signs
                    left[j][p * cells : (p + 1) * cells, :] = turned
                    turned_ref[c, p * cells : (p + 1) * cells, :] = turned
                    wide = sample.astype(F32)
                    part = wide[0:8]
                    for t in range(8, times, 8):
                        part = part + wide[t : t + 8]
                    sums_ref[row, one, p * cells : (p + 1) * cells] = (
                        jnp.sum(part * column_sign, axis=0, keepdims=True) * keep
                    )
                fill(right, u_ref[row, one, :], w_ref[row, one, :], column_ref, j * times, times)
            product = jnp.dot(join(left), join(right), preferred_element_type=F32)
            total = product if total is None else total + product
        acc_ref[...] += total
        return carry

    lax.fori_loop(0, channels // block, body, 0)
    finish(acc_ref, k_ref, sums_ref[...].reshape(channels, 2 * cells), out_ref, trials, scale)


def next_kernel(
    delays_ref, table_ref, column_ref, turned_ref, sums_ref, order_ref, out_ref,
    acc_ref, u_ref, w_ref, k_ref, *pairs, block, group, scale,
):
    channels, _, times = turned_ref.shape
    trials = delays_ref.shape[2]
    tiles = 2 * (trials // 128)
    prepare(delays_ref, table_ref, u_ref, w_ref, k_ref, channels, times)
    acc_ref[...] = jnp.zeros_like(acc_ref)

    def body(step, carry):
        total = None
        for i in range(block // group):
            right = pairs[i * tiles : (i + 1) * tiles]
            for j in range(group):
                at = i * group + j
                row = step * (block // 8) + at // 8
                one = slice(at % 8, at % 8 + 1)
                fill(right, u_ref[row, one, :], w_ref[row, one, :], column_ref, j * times, times)
            left = jnp.concatenate([turned_ref[step * block + i * group + j] for j in range(group)], axis=1)
            product = jnp.dot(left, join(right), preferred_element_type=F32)
            total = product if total is None else total + product
        acc_ref[...] += total
        return carry

    lax.fori_loop(0, channels // block, body, 0)
    finish(acc_ref, k_ref, sums_ref[...].reshape(channels, sums_ref.shape[2]), out_ref, trials, scale)


def working(trials, channels, cells):
    return [
        pltpu.VMEM((2 * cells, 2 * trials), F32),
        pltpu.VMEM((channels // 8, 8, trials), F32),
        pltpu.VMEM((channels // 8, 8, trials), F32),
        pltpu.VMEM((2 * channels, trials), F32),
    ]


def constants(times):
    table, column = time_tables(times)
    sign = np.where(np.arange(times) % 2 == 0, 1.0, -1.0).astype(np.float32)[None, :]
    return jnp.asarray(table), jnp.asarray(column), jnp.asarray(sign)


VMEM = pl.BlockSpec(memory_space=pltpu.VMEM)


def dedisperse_first(flags, delays, visibilities, scale):
    _, channels, times, cells = visibilities.shape
    trials = delays.shape[2]
    block, group = min(16, channels), 2
    scratch = working(trials, channels, cells)
    for _ in range(block // group):
        scratch += [pltpu.VMEM((group * times, 128), BF16)] * (2 * (trials // 128))
        scratch += [pltpu.VMEM((2 * cells, times), BF16)] * group
    return pl.pallas_call(
        functools.partial(first_kernel, block=block, group=group, scale=scale),
        in_specs=[pl.BlockSpec(memory_space=pltpu.SMEM)] + [VMEM] * 5,
        out_specs=[VMEM] * 3,
        out_shape=[
            jax.ShapeDtypeStruct((trials, 2 * cells), F32),
            jax.ShapeDtypeStruct((channels, 2 * cells, times), BF16),
            jax.ShapeDtypeStruct((channels // 8, 8, 2 * cells), F32),
        ],
        scratch_shapes=scratch,
        compiler_params=pltpu.CompilerParams(vmem_limit_bytes=24 << 20),
        cost_estimate=pl.CostEstimate(flops=10**10, bytes_accessed=20 << 20, transcendentals=0),
        name="dedisperse_first",
    )(flags, delays, *constants(times), visibilities)


def dedisperse_next(delays, turned, sums, order, scale):
    channels, cells, times = turned.shape
    cells //= 2
    trials = delays.shape[2]
    block, group = min(32, channels), 2
    scratch = working(trials, channels, cells)
    scratch += [pltpu.VMEM((group * times, 128), BF16)] * (2 * (trials // 128) * (block // group))
    table, column, _ = constants(times)
    return pl.pallas_call(
        functools.partial(next_kernel, block=block, group=group, scale=scale),
        in_specs=[VMEM] * 5 + [pl.BlockSpec(memory_space=pl.ANY)],
        out_specs=VMEM,
        out_shape=jax.ShapeDtypeStruct((trials, 2 * cells), F32),
        scratch_shapes=scratch,
        compiler_params=pltpu.CompilerParams(vmem_limit_bytes=24 << 20),
        cost_estimate=pl.CostEstimate(flops=10**10, bytes_accessed=20 << 20, transcendentals=0),
        name="dedisperse_next",
    )(delays, table, column, turned, sums, order)


def image_kernel(slot_ref, cos_ref, sin_ref, right_ref, *refs, side, weight):
    pieces, refs = refs[:-6], refs[-6:]
    image_ref, snr_ref, real_ref, imag_ref, peak_ref, power_ref = refs
    trials, cells = pieces[0].shape[0], pieces[0].shape[1] // 2
    for b, piece in enumerate(pieces):
        lanes = pl.ds(pl.multiple_of((slot_ref[0] ^ b) * cells, cells), cells)
        total = piece[...] * weight
        real_ref[:, lanes] = total[:, :cells]
        imag_ref[:, lanes] = total[:, cells:]
    right = right_ref[...]
    for d in range(trials):
        real = real_ref[d : d + 1, :]
        imag = imag_ref[d : d + 1, :]
        cosine, sine = cos_ref[...], sin_ref[...]
        first = real * cosine - imag * sine
        second = -(real * sine + imag * cosine)
        left = jnp.concatenate([first, second], axis=1)
        high = left.astype(BF16)
        low = (left - high.astype(F32)).astype(BF16)
        one = jnp.dot(jnp.concatenate([high, low], axis=0), right, preferred_element_type=F32)
        image = one[:side, :side] + (one[:side, side:] + one[side:, :side])
        image_ref[d] = image
        peak_ref[d : d + 1, :] = jnp.max(image, axis=0, keepdims=True)
        power_ref[d : d + 1, :] = jnp.sum(image * image, axis=0, keepdims=True)
    peak = jnp.max(peak_ref[...], axis=1, keepdims=True)
    power = jnp.sum(power_ref[...], axis=1, keepdims=True) / (side * side)
    snr_ref[...] = peak / jnp.sqrt(power + 1e-06)


def picture(pieces, slot, coord_u, coord_v, side, weight):
    total = coord_u.shape[0]
    trials = pieces[0].shape[0]
    pixels = jnp.arange(side, dtype=jnp.int32)
    row_angle = (pixels[:, None] * coord_u[None, :] % side).astype(F32) * (2.0 * math.pi / side)
    column_angle = (coord_v[:, None] * pixels[None, :] % side).astype(F32) * (2.0 * math.pi / side)
    columns = jnp.concatenate([jnp.cos(column_angle), jnp.sin(column_angle)], axis=0)
    high = lax.reduce_precision(columns, 8, 7)
    right = jnp.concatenate([high.astype(BF16), (columns - high).astype(BF16)], axis=1)
    images, snr = pl.pallas_call(
        functools.partial(image_kernel, side=side, weight=weight),
        in_specs=[pl.BlockSpec(memory_space=pltpu.SMEM)] + [VMEM] * (3 + len(pieces)),
        out_specs=[VMEM] * 2,
        out_shape=[jax.ShapeDtypeStruct((trials, side, side), F32), jax.ShapeDtypeStruct((trials, 1), F32)],
        scratch_shapes=[pltpu.VMEM((trials, total), F32)] * 2 + [pltpu.VMEM((trials, side), F32)] * 2,
        compiler_params=pltpu.CompilerParams(vmem_limit_bytes=40 << 20),
        name="picture",
    )(slot.reshape(1), jnp.cos(row_angle), jnp.sin(row_angle), right, *pieces)
    return images, snr[:, 0]


def swap(value, axes, size, step):
    return lax.ppermute(value, axes, [(i, i ^ step) for i in range(size)])


def shards(visibilities, flags, delays, coord_u, coord_v, *, sizes):
    channels, times = visibilities.shape[1:3]
    trials, total_channels = delays.shape
    near = sizes["pol"] * sizes["sub"]
    own = trials // sizes["uv"]
    position = lax.axis_index("uv")
    slot = lax.axis_index(("pol", "sub"))
    rows = lax.dynamic_slice_in_dim(delays, position * channels, channels, 1).T
    rows = rows.reshape(channels // 8, 8, trials)
    scale = 1.0 / math.sqrt(total_channels * times)
    weight = 2.0 / math.sqrt(coord_u.shape[0])
    if own % 128:
        part = dedisperse_first(flags, rows, visibilities, scale)[0]
        width = part.shape[1]
        part = part.reshape(sizes["uv"] * near, -1, width)
        held = lax.all_to_all(part, AXES, split_axis=0, concat_axis=0, tiled=True)
        held = held.reshape(sizes["uv"], near, -1, width).sum(axis=0)
        pieces = [lax.dynamic_index_in_dim(held, slot ^ i, 0, keepdims=False) for i in range(near)]
        return picture(pieces, slot, coord_u, coord_v, IMG, weight)

    def block(step):
        return lax.dynamic_slice_in_dim(rows, (position ^ step) * own, own, 2)

    last = sizes["uv"] - 1
    part, turned, sums = dedisperse_first(flags, block(last), visibilities, scale)
    held = [swap(part, "uv", sizes["uv"], last)]
    for step in range(last - 1, -1, -1):
        part = dedisperse_next(block(step), turned, sums, part, scale)
        if step:
            held.append(swap(part, "uv", sizes["uv"], step))
    for other in held:
        part = part + other
    part = part.reshape(near, own // near, part.shape[1])
    pieces = [lax.dynamic_index_in_dim(part, slot ^ i, 0, keepdims=False) for i in range(near)]
    pieces = [pieces[0]] + [swap(pieces[i], ("pol", "sub"), near, i) for i in range(1, near)]
    return picture(pieces, slot, coord_u, coord_v, IMG, weight)


def solution(mesh):
    in_specs = (P(None, "uv", "groups", ("pol", "sub")), P(("groups", "uv")), P(), P(), P())
    out_specs = (P(("groups", "uv", "pol", "sub"), None, None), P(("groups", "uv", "pol", "sub")))
    body = functools.partial(shards, sizes=dict(mesh.shape))
    return jax.shard_map(body, mesh=mesh, in_specs=in_specs, out_specs=out_specs, check_vma=False)
```

```python
import functools
import math

import jax
import jax.numpy as jnp
import numpy as np
from jax import lax
from jax.experimental import pallas as pl
from jax.experimental.pallas import tpu as pltpu
from jax.sharding import PartitionSpec as P

IMG = 128
FRAC = 8
AXES = ("uv", "pol", "sub")
F32 = jnp.float32
BF16 = jnp.bfloat16


def time_tables(times):
    t = np.arange(times)
    cot = np.where(t == 0, 2.0**60, 1.0 / np.tan(np.pi * np.where(t == 0, 1, t) / times))
    cot[times // 2] = 0.0
    cot = cot.astype(np.float32).astype(np.float64)
    power = 2.0 ** np.floor(16 - np.log2(np.maximum(np.abs(cot), 2.0**-10)))
    shifted = cot * power - np.where(t % 2 == 0, 1.0, -1.0) / times
    folded = np.minimum(t, times // 2)
    rows = [np.sin(np.pi * folded / times), np.cos(np.pi * folded / times), power, shifted]
    table = np.repeat(np.stack(rows), 8, axis=0)
    column = np.repeat(cot[:, None], times, axis=1)
    return np.concatenate([table, column]).astype(np.float32)


def coefficients(n, table_ref, times):
    cycle = FRAC * times
    height, width = n.shape
    lanes = table_ref.shape[1]
    fold = jnp.minimum(n, cycle - n)
    parts = []
    for i in range(4):
        index = (fold if i < 2 else n) >> 3
        source = table_ref[i * 8 : (i + 1) * 8, :]
        tiles = [
            [jnp.take_along_axis(source, index[r : r + 8, c : c + lanes], axis=1) for c in range(0, width, lanes)]
            for r in range(0, height, 8)
        ]
        parts.append(jnp.concatenate([jnp.concatenate(row, axis=1) for row in tiles], axis=0))
    sin_q, cos_q, power, shifted = parts
    theta = (fold & (FRAC - 1)).astype(F32) * (math.pi / cycle)
    square = theta * theta
    cos_r = 1.0 - square * (0.5 - square * (1.0 / 24.0))
    sin_r = theta * (1.0 - square * (1.0 / 6.0 - square * (1.0 / 120.0)))
    sin_a = sin_q * cos_r + cos_q * sin_r
    cos_a = cos_q * cos_r - sin_q * sin_r
    cos_a = jnp.where(n + n > cycle, -cos_a, cos_a)
    r = n & (FRAC - 1)
    side = jnp.abs(r - FRAC // 2)
    size = [math.cos(math.pi * i / FRAC) for i in range(FRAC // 2)]
    s = jnp.where(side == 0, size[0], jnp.where(side == 1, size[1], jnp.where(side == 2, size[2], size[3])))
    s = jnp.where((n & FRAC) == 0, s, -s)
    whole = r == 0
    ratio = sin_a / s
    u = jnp.where(whole, power, sin_a * ratio)
    w = jnp.where(whole, shifted, cos_a * ratio)
    k = jnp.where(whole, 0.0, s * cos_a / jnp.where(whole, 1.0, sin_a))
    return u, w, k, jnp.where(whole, 0.0, s)


def prepare(delays_ref, const_ref, u_ref, w_ref, k_ref, channels, times):
    trials = delays_ref.shape[2]
    many = math.gcd(4, channels // 8)

    def body(i, carry):
        rows = pl.ds(i * many, many)
        n = delays_ref[rows].reshape(many * 8, trials)
        u, w, k, s = coefficients(n, const_ref, times)
        u_ref[rows] = u.reshape(many, 8, trials)
        w_ref[rows] = w.reshape(many, 8, trials)
        size = many * 8
        k_ref[pl.ds(pl.multiple_of(i * size, 8), size), :] = k
        k_ref[pl.ds(pl.multiple_of(channels + i * size, 8), size), :] = s
        return carry

    lax.fori_loop(0, channels // 8 // many, body, 0)


def fill(right, u, w, const_ref, start, times):
    tiles = len(right) // 2
    for b in range(tiles):
        lanes = slice(b * 128, (b + 1) * 128)
        for t in range(0, times, 16):
            bottom = const_ref[32 + t : 48 + t, :] * u[:, lanes] - w[:, lanes]
            guess = pltpu.reciprocal(bottom, approx=True)
            high = guess.astype(BF16)
            rest = (1.0 - bottom * high.astype(F32)) * guess
            right[b][start + t : start + t + 16, :] = high
            right[tiles + b][start + t : start + t + 16, :] = rest.astype(BF16)


def join(refs):
    return jnp.concatenate([ref[...] for ref in refs], axis=1)


def finish(acc_ref, k_ref, sums, out_ref, trials, scale):
    cells = sums.shape[1] // 2
    real, imag = sums[:, :cells], sums[:, cells:]
    right = jnp.concatenate([sums, jnp.concatenate([imag, -real], axis=1)], axis=0)
    extra = jnp.dot(k_ref[...].T, right, precision=lax.Precision.HIGHEST, preferred_element_type=F32)
    main = (acc_ref[:, :trials] + acc_ref[:, trials:]).T
    out_ref[...] = (main + extra) * scale


def first_kernel(
    flags_hbm, const_hbm, delays_hbm, vis_hbm, out_ref, turned_ref, sums_ref, const_ref, *refs,
    block, group, copies, scale, blocks,
):
    _, channels, times, cells = vis_hbm.shape
    total, trials = delays_hbm.shape[0], out_ref.shape[0]
    later = [refs[i] for i in range(blocks - 1)]
    vis_ref, delays_ref, flags_ref, sem, side, first_ref, acc_ref, u_ref, w_ref, k_ref = refs[blocks - 1 : blocks + 9]
    pairs = refs[blocks + 9 :]
    tiles = 2 * (trials // 128)
    per = channels // copies
    at = lax.axis_index("uv") if blocks > 1 else 0
    lanes = pl.ds(pl.multiple_of(at * channels, channels), channels) if blocks > 1 else slice(None)
    small = [
        pltpu.make_async_copy(delays_hbm.at[:, lanes], delays_ref, side.at[0]),
        pltpu.make_async_copy(const_hbm, const_ref, side.at[1]),
        pltpu.make_async_copy(flags_hbm, flags_ref, side.at[2]),
    ]
    for copy in small:
        copy.start()

    def sample_copy(i, p):
        rows = pl.ds(i * per, per)
        return pltpu.make_async_copy(vis_hbm.at[p, rows], vis_ref.at[p, rows], sem.at[p, i])

    for i in range(copies):
        for p in range(2):
            sample_copy(i, p).start()
    acc_ref[...] = jnp.zeros_like(acc_ref)
    for copy in small:
        copy.wait()
    for step in range(blocks):
        mine = pl.ds(pl.multiple_of((at ^ step) * trials, trials), trials) if blocks > 1 else slice(None)
        turned = delays_ref[mine, :].T.reshape(channels // 8, 8, trials)
        (later[step] if step < blocks - 1 else first_ref)[...] = turned
    prepare(first_ref, const_ref, u_ref, w_ref, k_ref, channels, times)
    odd = lax.broadcasted_iota(jnp.int32, (1, times), 1) % 2
    sign_row = jnp.where(odd == 0, 1.0, -1.0)
    pick = lax.broadcasted_iota(jnp.int32, (16, times), 0)
    wide_sign = jnp.broadcast_to(sign_row, (16, times))

    def body(step, carry):
        total = None
        rows_sum = None
        for i in range(block // group):
            at = i * (tiles + group)
            right, left = pairs[at : at + tiles], pairs[at + tiles : at + tiles + group]
            picks = []
            for j in range(group):
                at = i * group + j
                c = step * block + at
                row = step * (block // 8) + at // 8
                one = slice(at % 8, at % 8 + 1)
                signs = (sign_row * flags_ref[c].astype(F32)).astype(BF16)
                for p in range(2):
                    turned = vis_ref[p, c].T * signs
                    left[j][p * cells : (p + 1) * cells, :] = turned
                    turned_ref[c, p * cells : (p + 1) * cells, :] = turned
                picks.append(jnp.where(pick == at, wide_sign, 0.0).astype(BF16))
                fill(right, u_ref[row, one, :], w_ref[row, one, :], const_ref, j * times, times)
            product = jnp.dot(join(left), join(right), preferred_element_type=F32)
            total = product if total is None else total + product
            here = pl.ds(step * block + i * group, group)
            natural = [vis_ref[p, here].reshape(group * times, cells) for p in range(2)]
            product = jnp.dot(
                jnp.concatenate(picks, axis=1), jnp.concatenate(natural, axis=1), preferred_element_type=F32
            )
            rows_sum = product if rows_sum is None else rows_sum + product
        acc_ref[...] += total
        for at in range(block):
            keep = flags_ref[step * block + at].astype(F32)
            sums_ref[step * (block // 8) + at // 8, at % 8 : at % 8 + 1, :] = rows_sum[at : at + 1, :] * keep
        return carry

    steps = channels // block // copies
    for i in range(copies):
        for p in range(2):
            sample_copy(i, p).wait()
        lax.fori_loop(i * steps, (i + 1) * steps, body, 0)
    finish(acc_ref, k_ref, sums_ref[...].reshape(channels, 2 * cells), out_ref, trials, scale)


def next_kernel(
    delays_ref, const_ref, turned_ref, sums_ref, order_ref, out_ref,
    acc_ref, u_ref, w_ref, k_ref, *pairs, block, group, scale,
):
    channels, _, times = turned_ref.shape
    trials = delays_ref.shape[2]
    tiles = 2 * (trials // 128)
    prepare(delays_ref, const_ref, u_ref, w_ref, k_ref, channels, times)
    acc_ref[...] = jnp.zeros_like(acc_ref)

    def body(step, carry):
        total = None
        for i in range(block // group):
            right = pairs[i * tiles : (i + 1) * tiles]
            for j in range(group):
                at = i * group + j
                row = step * (block // 8) + at // 8
                one = slice(at % 8, at % 8 + 1)
                fill(right, u_ref[row, one, :], w_ref[row, one, :], const_ref, j * times, times)
            left = jnp.concatenate([turned_ref[step * block + i * group + j] for j in range(group)], axis=1)
            product = jnp.dot(left, join(right), preferred_element_type=F32)
            total = product if total is None else total + product
        acc_ref[...] += total
        return carry

    lax.fori_loop(0, channels // block, body, 0)
    finish(acc_ref, k_ref, sums_ref[...].reshape(channels, sums_ref.shape[2]), out_ref, trials, scale)


def working(trials, channels, cells):
    return [
        pltpu.VMEM((2 * cells, 2 * trials), F32),
        pltpu.VMEM((channels // 8, 8, trials), F32),
        pltpu.VMEM((channels // 8, 8, trials), F32),
        pltpu.VMEM((2 * channels, trials), F32),
    ]


VMEM = pl.BlockSpec(memory_space=pltpu.VMEM)


def dedisperse_first(flags, delays, visibilities, scale, blocks):
    _, channels, times, cells = visibilities.shape
    trials = delays.shape[0] // blocks
    block, group = min(16, channels), 2
    copies = min(4, channels // block)
    table = time_tables(times)
    turned_delays = (channels // 8, 8, trials)
    scratch = [
        pltpu.VMEM(visibilities.shape, visibilities.dtype),
        pltpu.VMEM((delays.shape[0], channels), jnp.int32),
        pltpu.SMEM((channels,), jnp.int32),
        pltpu.SemaphoreType.DMA((2, copies)),
        pltpu.SemaphoreType.DMA((3,)),
        pltpu.VMEM(turned_delays, jnp.int32),
    ]
    scratch += working(trials, channels, cells)
    for _ in range(block // group):
        scratch += [pltpu.VMEM((group * times, 128), BF16)] * (2 * (trials // 128))
        scratch += [pltpu.VMEM((2 * cells, times), BF16)] * group
    hbm = pl.BlockSpec(memory_space=pltpu.HBM)
    return pl.pallas_call(
        functools.partial(first_kernel, block=block, group=group, copies=copies, scale=scale, blocks=blocks),
        in_specs=[hbm] * 4,
        out_specs=[VMEM] * (3 + blocks),
        out_shape=[
            jax.ShapeDtypeStruct((trials, 2 * cells), F32),
            jax.ShapeDtypeStruct((channels, 2 * cells, times), BF16),
            jax.ShapeDtypeStruct((channels // 8, 8, 2 * cells), F32),
            jax.ShapeDtypeStruct(table.shape, F32),
        ] + [jax.ShapeDtypeStruct(turned_delays, jnp.int32)] * (blocks - 1),
        scratch_shapes=scratch,
        compiler_params=pltpu.CompilerParams(vmem_limit_bytes=32 << 20),
        cost_estimate=pl.CostEstimate(flops=10**10, bytes_accessed=20 << 20, transcendentals=0),
        name="dedisperse_first",
    )(*[pltpu.with_memory_space_constraint(x, pltpu.HBM) for x in (flags, jnp.asarray(table), delays, visibilities)])


def dedisperse_next(delays, table, turned, sums, order, scale):
    channels, cells, times = turned.shape
    cells //= 2
    trials = delays.shape[2]
    block, group = min(32, channels), 2
    scratch = working(trials, channels, cells)
    scratch += [pltpu.VMEM((group * times, 128), BF16)] * (2 * (trials // 128) * (block // group))
    return pl.pallas_call(
        functools.partial(next_kernel, block=block, group=group, scale=scale),
        in_specs=[VMEM] * 4 + [pl.BlockSpec(memory_space=pl.ANY)],
        out_specs=VMEM,
        out_shape=jax.ShapeDtypeStruct((trials, 2 * cells), F32),
        scratch_shapes=scratch,
        compiler_params=pltpu.CompilerParams(vmem_limit_bytes=24 << 20),
        cost_estimate=pl.CostEstimate(flops=10**10, bytes_accessed=20 << 20, transcendentals=0),
        name="dedisperse_next",
    )(delays, table, turned, sums, order)


def image_kernel(slot_ref, cos_ref, sin_ref, right_ref, *refs, side, weight):
    pieces, refs = refs[:-6], refs[-6:]
    image_ref, snr_ref, real_ref, imag_ref, peak_ref, power_ref = refs
    trials, cells = pieces[0].shape[0], pieces[0].shape[1] // 2
    for b, piece in enumerate(pieces):
        lanes = pl.ds(pl.multiple_of((slot_ref[0] ^ b) * cells, cells), cells)
        total = piece[...] * weight
        real_ref[:, lanes] = total[:, :cells]
        imag_ref[:, lanes] = total[:, cells:]
    right = right_ref[...]
    for d in range(trials):
        real = real_ref[d : d + 1, :]
        imag = imag_ref[d : d + 1, :]
        cosine, sine = cos_ref[...], sin_ref[...]
        first = real * cosine - imag * sine
        second = -(real * sine + imag * cosine)
        left = jnp.concatenate([first, second], axis=1)
        high = left.astype(BF16)
        low = (left - high.astype(F32)).astype(BF16)
        one = jnp.dot(jnp.concatenate([high, low], axis=0), right, preferred_element_type=F32)
        image = one[:side, :side] + (one[:side, side:] + one[side:, :side])
        image_ref[d] = image
        peak_ref[d : d + 1, :] = jnp.max(image, axis=0, keepdims=True)
        power_ref[d : d + 1, :] = jnp.sum(image * image, axis=0, keepdims=True)
    peak = jnp.max(peak_ref[...], axis=1, keepdims=True)
    power = jnp.sum(power_ref[...], axis=1, keepdims=True) / (side * side)
    snr_ref[...] = peak / jnp.sqrt(power + 1e-06)


def picture(pieces, slot, coord_u, coord_v, side, weight):
    total = coord_u.shape[0]
    trials = pieces[0].shape[0]
    pixels = jnp.arange(side, dtype=jnp.int32)
    row_angle = (pixels[:, None] * coord_u[None, :] % side).astype(F32) * (2.0 * math.pi / side)
    column_angle = (coord_v[:, None] * pixels[None, :] % side).astype(F32) * (2.0 * math.pi / side)
    columns = jnp.concatenate([jnp.cos(column_angle), jnp.sin(column_angle)], axis=0)
    high = lax.reduce_precision(columns, 8, 7)
    right = jnp.concatenate([high.astype(BF16), (columns - high).astype(BF16)], axis=1)
    images, snr = pl.pallas_call(
        functools.partial(image_kernel, side=side, weight=weight),
        in_specs=[pl.BlockSpec(memory_space=pltpu.SMEM)] + [VMEM] * (3 + len(pieces)),
        out_specs=[VMEM] * 2,
        out_shape=[jax.ShapeDtypeStruct((trials, side, side), F32), jax.ShapeDtypeStruct((trials, 1), F32)],
        scratch_shapes=[pltpu.VMEM((trials, total), F32)] * 2 + [pltpu.VMEM((trials, side), F32)] * 2,
        compiler_params=pltpu.CompilerParams(vmem_limit_bytes=40 << 20),
        name="picture",
    )(slot.reshape(1), jnp.cos(row_angle), jnp.sin(row_angle), right, *pieces)
    return images, snr[:, 0]


def swap(value, axes, size, step):
    return lax.ppermute(value, axes, [(i, i ^ step) for i in range(size)])


def shards(visibilities, flags, delays, coord_u, coord_v, *, sizes):
    channels, times = visibilities.shape[1:3]
    trials, total_channels = delays.shape
    near = sizes["pol"] * sizes["sub"]
    own = trials // sizes["uv"]
    position = lax.axis_index("uv")
    slot = lax.axis_index(("pol", "sub"))
    scale = 1.0 / math.sqrt(total_channels * times)
    weight = 2.0 / math.sqrt(coord_u.shape[0])
    if own % 128 or channels % 128:
        rows = lax.dynamic_slice_in_dim(delays, position * channels, channels, 1)
        part = dedisperse_first(flags, rows, visibilities, scale, 1)[0]
        width = part.shape[1]
        part = part.reshape(sizes["uv"] * near, -1, width)
        held = lax.all_to_all(part, AXES, split_axis=0, concat_axis=0, tiled=True)
        held = held.reshape(sizes["uv"], near, -1, width).sum(axis=0)
        pieces = [lax.dynamic_index_in_dim(held, slot ^ i, 0, keepdims=False) for i in range(near)]
        return picture(pieces, slot, coord_u, coord_v, IMG, weight)

    last = sizes["uv"] - 1
    part, turned, sums, table, *rows = dedisperse_first(flags, delays, visibilities, scale, sizes["uv"])
    held = [swap(part, "uv", sizes["uv"], last)]
    for step in range(last - 1, -1, -1):
        part = dedisperse_next(rows[step], table, turned, sums, part, scale)
        if step:
            held.append(swap(part, "uv", sizes["uv"], step))
    for other in held:
        part = part + other
    part = part.reshape(near, own // near, part.shape[1])
    pieces = [lax.dynamic_index_in_dim(part, slot ^ i, 0, keepdims=False) for i in range(near)]
    pieces = [pieces[0]] + [swap(pieces[i], ("pol", "sub"), near, i) for i in range(1, near)]
    return picture(pieces, slot, coord_u, coord_v, IMG, weight)


def solution(mesh):
    in_specs = (P(None, "uv", "groups", ("pol", "sub")), P(("groups", "uv")), P(), P(), P())
    out_specs = (P(("groups", "uv", "pol", "sub"), None, None), P(("groups", "uv", "pol", "sub")))
    body = functools.partial(shards, sizes=dict(mesh.shape))
    return jax.shard_map(body, mesh=mesh, in_specs=in_specs, out_specs=out_specs, check_vma=False)
```

```python
import functools
import math

import jax
import jax.numpy as jnp
import numpy as np
from jax import lax
from jax.experimental import pallas as pl
from jax.experimental.pallas import tpu as pltpu
from jax.sharding import PartitionSpec as P

IMG = 128
FRAC = 8
AXES = ("uv", "pol", "sub")
F32 = jnp.float32
BF16 = jnp.bfloat16


def time_tables(times):
    t = np.arange(times)
    cot = np.where(t == 0, 2.0**60, 1.0 / np.tan(np.pi * np.where(t == 0, 1, t) / times))
    cot[times // 2] = 0.0
    cot = cot.astype(np.float32).astype(np.float64)
    power = 2.0 ** np.floor(16 - np.log2(np.maximum(np.abs(cot), 2.0**-10)))
    shifted = cot * power - np.where(t % 2 == 0, 1.0, -1.0) / times
    folded = np.minimum(t, times // 2)
    rows = [np.sin(np.pi * folded / times), np.cos(np.pi * folded / times), power, shifted]
    table = np.repeat(np.stack(rows), 8, axis=0)
    column = np.repeat(cot[:, None], times, axis=1)
    return np.concatenate([table, column]).astype(np.float32)


def coefficients(n, table_ref, times):
    cycle = FRAC * times
    height, width = n.shape
    lanes = table_ref.shape[1]
    fold = jnp.minimum(n, cycle - n)
    parts = []
    for i in range(4):
        index = (fold if i < 2 else n) >> 3
        source = table_ref[i * 8 : (i + 1) * 8, :]
        tiles = [
            [jnp.take_along_axis(source, index[r : r + 8, c : c + lanes], axis=1) for c in range(0, width, lanes)]
            for r in range(0, height, 8)
        ]
        parts.append(jnp.concatenate([jnp.concatenate(row, axis=1) for row in tiles], axis=0))
    sin_q, cos_q, power, shifted = parts
    theta = (fold & (FRAC - 1)).astype(F32) * (math.pi / cycle)
    square = theta * theta
    cos_r = 1.0 - square * (0.5 - square * (1.0 / 24.0))
    sin_r = theta * (1.0 - square * (1.0 / 6.0 - square * (1.0 / 120.0)))
    sin_a = sin_q * cos_r + cos_q * sin_r
    cos_a = cos_q * cos_r - sin_q * sin_r
    cos_a = jnp.where(n + n > cycle, -cos_a, cos_a)
    r = n & (FRAC - 1)
    side = jnp.abs(r - FRAC // 2)
    size = [math.cos(math.pi * i / FRAC) for i in range(FRAC // 2)]
    s = jnp.where(side == 0, size[0], jnp.where(side == 1, size[1], jnp.where(side == 2, size[2], size[3])))
    s = jnp.where((n & FRAC) == 0, s, -s)
    whole = r == 0
    ratio = sin_a / s
    u = jnp.where(whole, power, sin_a * ratio)
    w = jnp.where(whole, shifted, cos_a * ratio)
    k = jnp.where(whole, 0.0, s * cos_a / jnp.where(whole, 1.0, sin_a))
    return u, w, k, jnp.where(whole, 0.0, s)


def prepare(delays_ref, const_ref, u_ref, w_ref, k_ref, channels, times):
    trials = delays_ref.shape[2]
    many = math.gcd(4, channels // 8)

    def body(i, carry):
        rows = pl.ds(i * many, many)
        n = delays_ref[rows].reshape(many * 8, trials)
        u, w, k, s = coefficients(n, const_ref, times)
        u_ref[rows] = u.reshape(many, 8, trials)
        w_ref[rows] = w.reshape(many, 8, trials)
        size = many * 8
        k_ref[pl.ds(pl.multiple_of(i * size, 8), size), :] = k
        k_ref[pl.ds(pl.multiple_of(channels + i * size, 8), size), :] = s
        return carry

    lax.fori_loop(0, channels // 8 // many, body, 0)


def fill(right, u, w, const_ref, start, times):
    tiles = len(right) // 2
    for b in range(tiles):
        lanes = slice(b * 128, (b + 1) * 128)
        for t in range(0, times, 16):
            bottom = const_ref[32 + t : 48 + t, :] * u[:, lanes] - w[:, lanes]
            guess = pltpu.reciprocal(bottom, approx=True)
            high = guess.astype(BF16)
            rest = (1.0 - bottom * high.astype(F32)) * guess
            right[b][start + t : start + t + 16, :] = high
            right[tiles + b][start + t : start + t + 16, :] = rest.astype(BF16)


def join(refs):
    return jnp.concatenate([ref[...] for ref in refs], axis=1)


def finish(acc_ref, k_ref, sums, out_ref, trials, scale):
    cells = sums.shape[1] // 2
    real, imag = sums[:, :cells], sums[:, cells:]
    right = jnp.concatenate([sums, jnp.concatenate([imag, -real], axis=1)], axis=0)
    extra = jnp.dot(k_ref[...].T, right, precision=lax.Precision.HIGHEST, preferred_element_type=F32)
    main = (acc_ref[:, :trials] + acc_ref[:, trials:]).T
    out_ref[...] = (main + extra) * scale


def first_kernel(
    flags_hbm, const_hbm, delays_hbm, vis_hbm, out_ref, turned_ref, sums_ref, const_ref, *refs,
    block, group, copies, scale, blocks,
):
    _, channels, times, cells = vis_hbm.shape
    total, trials = delays_hbm.shape[0], out_ref.shape[0]
    later = [refs[i] for i in range(blocks - 1)]
    vis_ref, delays_ref, flags_ref, sem, side, first_ref, acc_ref, u_ref, w_ref, k_ref = refs[blocks - 1 : blocks + 9]
    pairs = refs[blocks + 9 :]
    tiles = 2 * (trials // 128)
    per = channels // copies
    at = lax.axis_index("uv") if blocks > 1 else 0
    lanes = pl.ds(pl.multiple_of(at * channels, channels), channels) if blocks > 1 else slice(None)
    small = [
        pltpu.make_async_copy(delays_hbm.at[:, lanes], delays_ref, side.at[0]),
        pltpu.make_async_copy(const_hbm, const_ref, side.at[1]),
        pltpu.make_async_copy(flags_hbm, flags_ref, side.at[2]),
    ]
    for copy in small:
        copy.start()

    def sample_copy(i, p):
        rows = pl.ds(i * per, per)
        return pltpu.make_async_copy(vis_hbm.at[p, rows], vis_ref.at[p, rows], sem.at[p, i])

    for i in range(copies):
        for p in range(2):
            sample_copy(i, p).start()
    acc_ref[...] = jnp.zeros_like(acc_ref)
    for copy in small:
        copy.wait()
    for step in range(blocks):
        mine = pl.ds(pl.multiple_of((at ^ step) * trials, trials), trials) if blocks > 1 else slice(None)
        turned = delays_ref[mine, :].T.reshape(channels // 8, 8, trials)
        (later[step] if step < blocks - 1 else first_ref)[...] = turned
    prepare(first_ref, const_ref, u_ref, w_ref, k_ref, channels, times)
    odd = lax.broadcasted_iota(jnp.int32, (1, times), 1) % 2
    sign_row = jnp.where(odd == 0, 1.0, -1.0)
    pick = lax.broadcasted_iota(jnp.int32, (16, times), 0)
    wide_sign = jnp.broadcast_to(sign_row, (16, times))

    def body(step, carry):
        total = None
        rows_sum = None
        for i in range(block // group):
            at = i * (tiles + group)
            right, left = pairs[at : at + tiles], pairs[at + tiles : at + tiles + group]
            picks = []
            for j in range(group):
                at = i * group + j
                c = step * block + at
                row = step * (block // 8) + at // 8
                one = slice(at % 8, at % 8 + 1)
                signs = (sign_row * flags_ref[c].astype(F32)).astype(BF16)
                for p in range(2):
                    turned = vis_ref[p, c].T * signs
                    left[j][p * cells : (p + 1) * cells, :] = turned
                    turned_ref[c, p * cells : (p + 1) * cells, :] = turned
                picks.append(jnp.where(pick == at, wide_sign, 0.0).astype(BF16))
                fill(right, u_ref[row, one, :], w_ref[row, one, :], const_ref, j * times, times)
            product = jnp.dot(join(left), join(right), preferred_element_type=F32)
            total = product if total is None else total + product
            here = pl.ds(step * block + i * group, group)
            natural = [vis_ref[p, here].reshape(group * times, cells) for p in range(2)]
            product = jnp.dot(
                jnp.concatenate(picks, axis=1), jnp.concatenate(natural, axis=1), preferred_element_type=F32
            )
            rows_sum = product if rows_sum is None else rows_sum + product
        acc_ref[...] += total
        for at in range(block):
            keep = flags_ref[step * block + at].astype(F32)
            sums_ref[step * (block // 8) + at // 8, at % 8 : at % 8 + 1, :] = rows_sum[at : at + 1, :] * keep
        return carry

    steps = channels // block // copies
    for i in range(copies):
        for p in range(2):
            sample_copy(i, p).wait()
        lax.fori_loop(i * steps, (i + 1) * steps, body, 0)
    finish(acc_ref, k_ref, sums_ref[...].reshape(channels, 2 * cells), out_ref, trials, scale)


def next_kernel(
    delays_ref, const_ref, turned_ref, sums_ref, order_ref, out_ref,
    acc_ref, u_ref, w_ref, k_ref, *pairs, block, group, scale,
):
    channels, _, times = turned_ref.shape
    trials = delays_ref.shape[2]
    tiles = 2 * (trials // 128)
    prepare(delays_ref, const_ref, u_ref, w_ref, k_ref, channels, times)
    acc_ref[...] = jnp.zeros_like(acc_ref)

    def body(step, carry):
        total = None
        for i in range(block // group):
            right = pairs[i * tiles : (i + 1) * tiles]
            for j in range(group):
                at = i * group + j
                row = step * (block // 8) + at // 8
                one = slice(at % 8, at % 8 + 1)
                fill(right, u_ref[row, one, :], w_ref[row, one, :], const_ref, j * times, times)
            left = jnp.concatenate([turned_ref[step * block + i * group + j] for j in range(group)], axis=1)
            product = jnp.dot(left, join(right), preferred_element_type=F32)
            total = product if total is None else total + product
        acc_ref[...] += total
        return carry

    lax.fori_loop(0, channels // block, body, 0)
    finish(acc_ref, k_ref, sums_ref[...].reshape(channels, sums_ref.shape[2]), out_ref, trials, scale)


def working(trials, channels, cells):
    return [
        pltpu.VMEM((2 * cells, 2 * trials), F32),
        pltpu.VMEM((channels // 8, 8, trials), F32),
        pltpu.VMEM((channels // 8, 8, trials), F32),
        pltpu.VMEM((2 * channels, trials), F32),
    ]


VMEM = pl.BlockSpec(memory_space=pltpu.VMEM)


def dedisperse_first(flags, delays, visibilities, scale, blocks):
    _, channels, times, cells = visibilities.shape
    trials = delays.shape[0] // blocks
    block, group = min(16, channels), 2
    copies = min(4, channels // block)
    table = time_tables(times)
    turned_delays = (channels // 8, 8, trials)
    scratch = [
        pltpu.VMEM(visibilities.shape, visibilities.dtype),
        pltpu.VMEM((delays.shape[0], channels), jnp.int32),
        pltpu.SMEM((channels,), jnp.int32),
        pltpu.SemaphoreType.DMA((2, copies)),
        pltpu.SemaphoreType.DMA((3,)),
        pltpu.VMEM(turned_delays, jnp.int32),
    ]
    scratch += working(trials, channels, cells)
    for _ in range(block // group):
        scratch += [pltpu.VMEM((group * times, 128), BF16)] * (2 * (trials // 128))
        scratch += [pltpu.VMEM((2 * cells, times), BF16)] * group
    hbm = pl.BlockSpec(memory_space=pltpu.HBM)
    return pl.pallas_call(
        functools.partial(first_kernel, block=block, group=group, copies=copies, scale=scale, blocks=blocks),
        in_specs=[hbm] * 4,
        out_specs=[VMEM] * (3 + blocks),
        out_shape=[
            jax.ShapeDtypeStruct((trials, 2 * cells), F32),
            jax.ShapeDtypeStruct((channels, 2 * cells, times), BF16),
            jax.ShapeDtypeStruct((channels // 8, 8, 2 * cells), F32),
            jax.ShapeDtypeStruct(table.shape, F32),
        ] + [jax.ShapeDtypeStruct(turned_delays, jnp.int32)] * (blocks - 1),
        scratch_shapes=scratch,
        compiler_params=pltpu.CompilerParams(vmem_limit_bytes=32 << 20),
        cost_estimate=pl.CostEstimate(flops=10**10, bytes_accessed=20 << 20, transcendentals=0),
        name="dedisperse_first",
    )(*[pltpu.with_memory_space_constraint(x, pltpu.HBM) for x in (flags, jnp.asarray(table), delays, visibilities)])


def dedisperse_next(delays, table, turned, sums, order, scale):
    channels, cells, times = turned.shape
    cells //= 2
    trials = delays.shape[2]
    block, group = min(32, channels), 2
    scratch = working(trials, channels, cells)
    scratch += [pltpu.VMEM((group * times, 128), BF16)] * (2 * (trials // 128) * (block // group))
    return pl.pallas_call(
        functools.partial(next_kernel, block=block, group=group, scale=scale),
        in_specs=[VMEM] * 4 + [pl.BlockSpec(memory_space=pl.ANY)],
        out_specs=VMEM,
        out_shape=jax.ShapeDtypeStruct((trials, 2 * cells), F32),
        scratch_shapes=scratch,
        compiler_params=pltpu.CompilerParams(vmem_limit_bytes=24 << 20),
        cost_estimate=pl.CostEstimate(flops=10**10, bytes_accessed=20 << 20, transcendentals=0),
        name="dedisperse_next",
    )(delays, table, turned, sums, order)


def wave_tables(side):
    angle = 2.0 * np.pi / side * np.arange(side)
    wave = np.repeat(np.stack([np.cos(angle), np.sin(angle)]), 8, axis=0).astype(np.float32)
    half = side // 2
    index = np.arange(half)[:, None] * np.arange(side)[None, :] % side
    cosine, sine = np.cos(angle)[index], np.sin(angle)[index]
    even = np.block([[cosine, cosine], [cosine, -cosine], [-sine, -sine], [-sine, sine]])
    odd = np.block([[cosine, cosine], [-sine, sine], [-sine, -sine], [-cosine, cosine]])
    stacked = []
    for matrix in (even, odd):
        high = matrix.astype(jnp.bfloat16)
        low = (matrix - high.astype(np.float64)).astype(jnp.bfloat16)
        stacked.append(np.concatenate([high, high, low], axis=0))
    return wave, np.stack(stacked)


def cell_kernel(u_ref, v_ref, wave_ref, order_ref, cos_ref, sin_ref, hot_ref, *, side):
    lanes = wave_ref.shape[1]
    u = u_ref[...]
    for r in range(0, side // 4, 8):
        row = lax.broadcasted_iota(jnp.int32, (8, lanes), 0) + r
        for c in range(0, u.shape[1], lanes):
            index = row * u[:, c : c + lanes] % side
            cos_ref[r : r + 8, c : c + lanes] = jnp.take_along_axis(wave_ref[0:8, :], index, axis=1)
            sin_ref[r : r + 8, c : c + lanes] = jnp.take_along_axis(wave_ref[8:16, :], index, axis=1)
    code = (u & 3) * (side // 2) + v_ref[...]
    rows = lax.broadcasted_iota(jnp.int32, hot_ref.shape, 0)
    hot_ref[...] = jnp.where(rows == code, 1.0, 0.0).astype(BF16)


def split(value):
    high = value.astype(BF16)
    return high, (value - high.astype(F32)).astype(BF16)


def image_kernel(slot_ref, cos_ref, sin_ref, hot_ref, last_ref, *refs, side, weight, batch):
    pieces, refs = refs[:-7], refs[-7:]
    image_ref, snr_ref, real_ref, imag_ref, left_ref, peak_ref, power_ref = refs
    trials, cells = pieces[0].shape[0], pieces[0].shape[1] // 2
    total = real_ref.shape[2]
    quarter = side // 4
    for b, piece in enumerate(pieces):
        lanes = pl.ds(pl.multiple_of((slot_ref[0] ^ b) * cells, cells), cells)
        value = (piece[...] * weight).reshape(trials // batch, batch, 2 * cells)
        real_ref[:, :, lanes] = value[:, :, :cells]
        imag_ref[:, :, lanes] = value[:, :, cells:]

    def body(step, carry):
        for i in range(batch):
            real, imag = real_ref[step, i : i + 1, :], imag_ref[step, i : i + 1, :]
            cosine, sine = cos_ref[...], sin_ref[...]
            for part, value in enumerate((real * cosine - imag * sine, real * sine + imag * cosine)):
                rows = slice((2 * i + part) * quarter, (2 * i + part + 1) * quarter)
                left_ref[rows, :total], left_ref[rows, total:] = split(value)
        hot = hot_ref[...]
        sums = lax.dot_general(
            left_ref[...], jnp.concatenate([hot, hot], axis=1), (((1,), (1,)), ((), ())),
            preferred_element_type=F32,
        )
        first, second = sums[:, :side], sums[:, side:]
        found = []
        for which, value in enumerate((first + second, first - second)):
            value = value.reshape(batch, 2, quarter, side)
            value = jnp.concatenate([value[:, 0], value[:, 1]], axis=2).reshape(batch * quarter, 2 * side)
            high, low = split(value)
            left = jnp.concatenate([high, low, high], axis=1)
            found.append(jnp.dot(left, last_ref[which], preferred_element_type=F32))
        for i in range(batch):
            peak, power = None, None
            for q in range(4):
                half = slice(side * (q // 2), side * (q // 2 + 1))
                tile = found[q % 2][i * quarter : (i + 1) * quarter, half]
                image_ref[step * batch + i, q * quarter : (q + 1) * quarter, :] = tile
                peak = tile if q == 0 else jnp.maximum(peak, tile)
                power = tile * tile if q == 0 else power + tile * tile
            peak_ref[step, i : i + 1, :] = jnp.max(peak, axis=0, keepdims=True)
            power_ref[step, i : i + 1, :] = jnp.sum(power, axis=0, keepdims=True)
        return carry

    lax.fori_loop(0, trials // batch, body, 0)
    peak = jnp.max(peak_ref[...].reshape(trials, side), axis=1, keepdims=True)
    power = jnp.sum(power_ref[...].reshape(trials, side), axis=1, keepdims=True) / (side * side)
    snr = peak / jnp.sqrt(power + 1e-06)
    corner = lax.broadcasted_iota(jnp.int32, (trials, trials), 0) == lax.broadcasted_iota(jnp.int32, (trials, trials), 1)
    snr_ref[...] = jnp.sum(jnp.where(corner, snr, 0.0), axis=0, keepdims=True)


def cell_tables(coord_u, coord_v, order, side):
    total = coord_u.shape[0]
    wave, _ = wave_tables(side)
    return pl.pallas_call(
        functools.partial(cell_kernel, side=side),
        in_specs=[VMEM] * 3 + [pl.BlockSpec(memory_space=pl.ANY)],
        out_specs=[VMEM] * 3,
        out_shape=[jax.ShapeDtypeStruct((side // 4, total), F32)] * 2 + [jax.ShapeDtypeStruct((2 * side, total), BF16)],
        compiler_params=pltpu.CompilerParams(vmem_limit_bytes=16 << 20),
        cost_estimate=pl.CostEstimate(flops=10**9, bytes_accessed=1 << 20, transcendentals=0),
        name="cell_tables",
    )(coord_u.reshape(1, total), coord_v.reshape(1, total), jnp.asarray(wave), order)


def picture(pieces, slot, cells, side, weight):
    trials = pieces[0].shape[0]
    total = cells[0].shape[1]
    batch = math.gcd(8, trials)
    _, last = wave_tables(side)
    images, snr = pl.pallas_call(
        functools.partial(image_kernel, side=side, weight=weight, batch=batch),
        in_specs=[pl.BlockSpec(memory_space=pltpu.SMEM)] + [VMEM] * (4 + len(pieces)),
        out_specs=[VMEM] * 2,
        out_shape=[jax.ShapeDtypeStruct((trials, side, side), F32), jax.ShapeDtypeStruct((1, trials), F32)],
        scratch_shapes=[pltpu.VMEM((trials // batch, batch, total), F32)] * 2
        + [pltpu.VMEM((batch * side // 2, 2 * total), BF16)]
        + [pltpu.VMEM((trials // batch, batch, side), F32)] * 2,
        compiler_params=pltpu.CompilerParams(vmem_limit_bytes=32 << 20),
        name="picture",
    )(slot.reshape(1), *cells, jnp.asarray(last), *pieces)
    return images, snr.reshape(trials)


def swap(value, axes, size, step):
    return lax.ppermute(value, axes, [(i, i ^ step) for i in range(size)])


def shards(visibilities, flags, delays, coord_u, coord_v, *, sizes):
    channels, times = visibilities.shape[1:3]
    trials, total_channels = delays.shape
    near = sizes["pol"] * sizes["sub"]
    own = trials // sizes["uv"]
    position = lax.axis_index("uv")
    slot = lax.axis_index(("pol", "sub"))
    scale = 1.0 / math.sqrt(total_channels * times)
    weight = 2.0 / math.sqrt(coord_u.shape[0])
    if own % 128 or channels % 128:
        rows = lax.dynamic_slice_in_dim(delays, position * channels, channels, 1)
        part = dedisperse_first(flags, rows, visibilities, scale, 1)[0]
        width = part.shape[1]
        part = part.reshape(sizes["uv"] * near, -1, width)
        held = lax.all_to_all(part, AXES, split_axis=0, concat_axis=0, tiled=True)
        held = held.reshape(sizes["uv"], near, -1, width).sum(axis=0)
        pieces = [lax.dynamic_index_in_dim(held, slot ^ i, 0, keepdims=False) for i in range(near)]
        return picture(pieces, slot, cell_tables(coord_u, coord_v, part, IMG), IMG, weight)

    last = sizes["uv"] - 1
    part, turned, sums, table, *rows = dedisperse_first(flags, delays, visibilities, scale, sizes["uv"])
    held = [swap(part, "uv", sizes["uv"], last)]
    for step in range(last - 1, -1, -1):
        part = dedisperse_next(rows[step], table, turned, sums, part, scale)
        if step:
            held.append(swap(part, "uv", sizes["uv"], step))
    for other in held:
        part = part + other
    cells = cell_tables(coord_u, coord_v, part, IMG)
    part = part.reshape(near, own // near, part.shape[1])
    pieces = [lax.dynamic_index_in_dim(part, slot ^ i, 0, keepdims=False) for i in range(near)]
    pieces = [pieces[0]] + [swap(pieces[i], ("pol", "sub"), near, i) for i in range(1, near)]
    return picture(pieces, slot, cells, IMG, weight)


def solution(mesh):
    in_specs = (P(None, "uv", "groups", ("pol", "sub")), P(("groups", "uv")), P(), P(), P())
    out_specs = (P(("groups", "uv", "pol", "sub"), None, None), P(("groups", "uv", "pol", "sub")))
    body = functools.partial(shards, sizes=dict(mesh.shape))
    return jax.shard_map(body, mesh=mesh, in_specs=in_specs, out_specs=out_specs, check_vma=False)
```

```python
import functools
import math

import jax
import jax.numpy as jnp
import numpy as np
from jax import lax
from jax.experimental import pallas as pl
from jax.experimental.pallas import tpu as pltpu
from jax.sharding import PartitionSpec as P

IMG = 128
FRAC = 8
AXES = ("uv", "pol", "sub")
F32 = jnp.float32
BF16 = jnp.bfloat16


def time_tables(times):
    t = np.arange(times)
    cot = np.where(t == 0, 2.0**60, 1.0 / np.tan(np.pi * np.where(t == 0, 1, t) / times))
    cot[times // 2] = 0.0
    cot = cot.astype(np.float32).astype(np.float64)
    power = 2.0 ** np.floor(16 - np.log2(np.maximum(np.abs(cot), 2.0**-10)))
    shifted = cot * power - np.where(t % 2 == 0, 1.0, -1.0) / times
    folded = np.minimum(t, times // 2)
    rows = [np.sin(np.pi * folded / times), np.cos(np.pi * folded / times), power, shifted]
    table = np.repeat(np.stack(rows), 8, axis=0)
    column = np.repeat(cot[:, None], times, axis=1)
    return np.concatenate([table, column]).astype(np.float32)


def coefficients(n, table_ref, times):
    cycle = FRAC * times
    height, width = n.shape
    lanes = table_ref.shape[1]
    fold = jnp.minimum(n, cycle - n)
    parts = []
    for i in range(4):
        index = (fold if i < 2 else n) >> 3
        source = table_ref[i * 8 : (i + 1) * 8, :]
        tiles = [
            [jnp.take_along_axis(source, index[r : r + 8, c : c + lanes], axis=1) for c in range(0, width, lanes)]
            for r in range(0, height, 8)
        ]
        parts.append(jnp.concatenate([jnp.concatenate(row, axis=1) for row in tiles], axis=0))
    sin_q, cos_q, power, shifted = parts
    theta = (fold & (FRAC - 1)).astype(F32) * (math.pi / cycle)
    square = theta * theta
    cos_r = 1.0 - square * (0.5 - square * (1.0 / 24.0))
    sin_r = theta * (1.0 - square * (1.0 / 6.0 - square * (1.0 / 120.0)))
    sin_a = sin_q * cos_r + cos_q * sin_r
    cos_a = cos_q * cos_r - sin_q * sin_r
    cos_a = jnp.where(n + n > cycle, -cos_a, cos_a)
    r = n & (FRAC - 1)
    side = jnp.abs(r - FRAC // 2)
    size = [math.cos(math.pi * i / FRAC) for i in range(FRAC // 2)]
    s = jnp.where(side == 0, size[0], jnp.where(side == 1, size[1], jnp.where(side == 2, size[2], size[3])))
    s = jnp.where((n & FRAC) == 0, s, -s)
    whole = r == 0
    ratio = sin_a / s
    u = jnp.where(whole, power, sin_a * ratio)
    w = jnp.where(whole, shifted, cos_a * ratio)
    k = jnp.where(whole, 0.0, s * cos_a / jnp.where(whole, 1.0, sin_a))
    return u, w, k, jnp.where(whole, 0.0, s)


def prepare(delays_ref, const_ref, u_ref, w_ref, k_ref, channels, times):
    trials = delays_ref.shape[2]
    many = math.gcd(4, channels // 8)

    def body(i, carry):
        rows = pl.ds(i * many, many)
        n = delays_ref[rows].reshape(many * 8, trials)
        u, w, k, s = coefficients(n, const_ref, times)
        u_ref[rows] = u.reshape(many, 8, trials)
        w_ref[rows] = w.reshape(many, 8, trials)
        size = many * 8
        k_ref[pl.ds(pl.multiple_of(i * size, 8), size), :] = k
        k_ref[pl.ds(pl.multiple_of(channels + i * size, 8), size), :] = s
        return carry

    lax.fori_loop(0, channels // 8 // many, body, 0)


def fill(right, u, w, const_ref, start, times):
    tiles = len(right) // 2
    for b in range(tiles):
        lanes = slice(b * 128, (b + 1) * 128)
        for t in range(0, times, 16):
            bottom = const_ref[32 + t : 48 + t, :] * u[:, lanes] - w[:, lanes]
            guess = pltpu.reciprocal(bottom, approx=True)
            high = guess.astype(BF16)
            rest = (1.0 - bottom * high.astype(F32)).astype(BF16) * high
            right[b][start + t : start + t + 16, :] = high
            right[tiles + b][start + t : start + t + 16, :] = rest


def join(refs):
    return jnp.concatenate([ref[...] for ref in refs], axis=1)


def finish(acc_ref, k_ref, sums, out_ref, trials, scale):
    cells = sums.shape[1] // 2
    real, imag = sums[:, :cells], sums[:, cells:]
    right = jnp.concatenate([sums, jnp.concatenate([imag, -real], axis=1)], axis=0)
    extra = jnp.dot(k_ref[...].T, right, precision=lax.Precision.HIGHEST, preferred_element_type=F32)
    main = (acc_ref[:, :trials] + acc_ref[:, trials:]).T
    out_ref[...] = (main + extra) * scale


def first_kernel(
    flags_hbm, const_hbm, delays_hbm, vis_hbm, out_ref, turned_ref, sums_ref, const_ref, *refs,
    block, group, copies, scale, blocks,
):
    _, channels, times, cells = vis_hbm.shape
    total, trials = delays_hbm.shape[0], out_ref.shape[0]
    later = [refs[i] for i in range(blocks - 1)]
    vis_ref, delays_ref, flags_ref, sem, side, first_ref, acc_ref, u_ref, w_ref, k_ref = refs[blocks - 1 : blocks + 9]
    pairs = refs[blocks + 9 :]
    tiles = 2 * (trials // 128)
    per = channels // copies
    at = lax.axis_index("uv") if blocks > 1 else 0
    lanes = pl.ds(pl.multiple_of(at * channels, channels), channels) if blocks > 1 else slice(None)
    small = [
        pltpu.make_async_copy(delays_hbm.at[:, lanes], delays_ref, side.at[0]),
        pltpu.make_async_copy(const_hbm, const_ref, side.at[1]),
        pltpu.make_async_copy(flags_hbm, flags_ref, side.at[2]),
    ]
    for copy in small:
        copy.start()

    def sample_copy(i, p):
        rows = pl.ds(i * per, per)
        return pltpu.make_async_copy(vis_hbm.at[p, rows], vis_ref.at[p, rows], sem.at[p, i])

    for i in range(copies):
        for p in range(2):
            sample_copy(i, p).start()
    acc_ref[...] = jnp.zeros_like(acc_ref)
    for copy in small:
        copy.wait()
    for step in range(blocks):
        mine = pl.ds(pl.multiple_of((at ^ step) * trials, trials), trials) if blocks > 1 else slice(None)
        turned = delays_ref[mine, :].T.reshape(channels // 8, 8, trials)
        (later[step] if step < blocks - 1 else first_ref)[...] = turned
    prepare(first_ref, const_ref, u_ref, w_ref, k_ref, channels, times)
    odd = lax.broadcasted_iota(jnp.int32, (1, times), 1) % 2
    sign_row = jnp.where(odd == 0, 1.0, -1.0)
    height = max(16, block)
    pick = lax.broadcasted_iota(jnp.int32, (height, times), 0)
    wide_sign = jnp.broadcast_to(sign_row, (height, times))

    def body(step, carry):
        for p in range(2):
            sample_copy(step, p).wait()
        total = None
        rows_sum = None
        for i in range(block // group):
            right = pairs[i * tiles : (i + 1) * tiles]
            picks = []
            for j in range(group):
                at = i * group + j
                c = step * block + at
                row = step * (block // 8) + at // 8
                one = slice(at % 8, at % 8 + 1)
                signs = (sign_row * flags_ref[c].astype(F32)).astype(BF16)
                for p in range(2):
                    turned = vis_ref[p, c].T * signs
                    turned_ref[c, p * cells : (p + 1) * cells, :] = turned
                picks.append(jnp.where(pick == at, wide_sign, 0.0).astype(BF16))
                fill(right, u_ref[row, one, :], w_ref[row, one, :], const_ref, j * times, times)
            left = jnp.concatenate([turned_ref[step * block + i * group + j] for j in range(group)], axis=1)
            product = jnp.dot(left, join(right), preferred_element_type=F32)
            total = product if total is None else total + product
            here = pl.ds(step * block + i * group, group)
            natural = [vis_ref[p, here].reshape(group * times, cells) for p in range(2)]
            product = jnp.dot(
                jnp.concatenate(picks, axis=1), jnp.concatenate(natural, axis=1), preferred_element_type=F32
            )
            rows_sum = product if rows_sum is None else rows_sum + product
        acc_ref[...] += total
        for at in range(block):
            keep = flags_ref[step * block + at].astype(F32)
            sums_ref[step * (block // 8) + at // 8, at % 8 : at % 8 + 1, :] = rows_sum[at : at + 1, :] * keep
        return carry

    lax.fori_loop(0, copies, body, 0)
    finish(acc_ref, k_ref, sums_ref[...].reshape(channels, 2 * cells), out_ref, trials, scale)


def next_kernel(
    delays_ref, const_ref, turned_ref, sums_ref, order_ref, out_ref,
    acc_ref, u_ref, w_ref, k_ref, *pairs, block, group, scale,
):
    channels, _, times = turned_ref.shape
    trials = delays_ref.shape[2]
    tiles = 2 * (trials // 128)
    prepare(delays_ref, const_ref, u_ref, w_ref, k_ref, channels, times)
    acc_ref[...] = jnp.zeros_like(acc_ref)

    def body(step, carry):
        total = None
        for i in range(block // group):
            right = pairs[i * tiles : (i + 1) * tiles]
            for j in range(group):
                at = i * group + j
                row = step * (block // 8) + at // 8
                one = slice(at % 8, at % 8 + 1)
                fill(right, u_ref[row, one, :], w_ref[row, one, :], const_ref, j * times, times)
            left = jnp.concatenate([turned_ref[step * block + i * group + j] for j in range(group)], axis=1)
            product = jnp.dot(left, join(right), preferred_element_type=F32)
            total = product if total is None else total + product
        acc_ref[...] += total
        return carry

    lax.fori_loop(0, channels // block, body, 0)
    finish(acc_ref, k_ref, sums_ref[...].reshape(channels, sums_ref.shape[2]), out_ref, trials, scale)


def working(trials, channels, cells):
    return [
        pltpu.VMEM((2 * cells, 2 * trials), F32),
        pltpu.VMEM((channels // 8, 8, trials), F32),
        pltpu.VMEM((channels // 8, 8, trials), F32),
        pltpu.VMEM((2 * channels, trials), F32),
    ]


VMEM = pl.BlockSpec(memory_space=pltpu.VMEM)


def dedisperse_first(flags, delays, visibilities, scale, blocks):
    _, channels, times, cells = visibilities.shape
    trials = delays.shape[0] // blocks
    block, group = min(32, channels), 2
    copies = channels // block
    table = time_tables(times)
    turned_delays = (channels // 8, 8, trials)
    scratch = [
        pltpu.VMEM(visibilities.shape, visibilities.dtype),
        pltpu.VMEM((delays.shape[0], channels), jnp.int32),
        pltpu.SMEM((channels,), jnp.int32),
        pltpu.SemaphoreType.DMA((2, copies)),
        pltpu.SemaphoreType.DMA((3,)),
        pltpu.VMEM(turned_delays, jnp.int32),
    ]
    scratch += working(trials, channels, cells)
    for _ in range(block // group):
        scratch += [pltpu.VMEM((group * times, 128), BF16)] * (2 * (trials // 128))
    hbm = pl.BlockSpec(memory_space=pltpu.HBM)
    return pl.pallas_call(
        functools.partial(first_kernel, block=block, group=group, copies=copies, scale=scale, blocks=blocks),
        in_specs=[hbm] * 4,
        out_specs=[VMEM] * (3 + blocks),
        out_shape=[
            jax.ShapeDtypeStruct((trials, 2 * cells), F32),
            jax.ShapeDtypeStruct((channels, 2 * cells, times), BF16),
            jax.ShapeDtypeStruct((channels // 8, 8, 2 * cells), F32),
            jax.ShapeDtypeStruct(table.shape, F32),
        ] + [jax.ShapeDtypeStruct(turned_delays, jnp.int32)] * (blocks - 1),
        scratch_shapes=scratch,
        compiler_params=pltpu.CompilerParams(vmem_limit_bytes=32 << 20),
        cost_estimate=pl.CostEstimate(flops=10**10, bytes_accessed=20 << 20, transcendentals=0),
        name="dedisperse_first",
    )(*[pltpu.with_memory_space_constraint(x, pltpu.HBM) for x in (flags, jnp.asarray(table), delays, visibilities)])


def dedisperse_next(delays, table, turned, sums, order, scale):
    channels, cells, times = turned.shape
    cells //= 2
    trials = delays.shape[2]
    block, group = min(32, channels), 2
    scratch = working(trials, channels, cells)
    scratch += [pltpu.VMEM((group * times, 128), BF16)] * (2 * (trials // 128) * (block // group))
    return pl.pallas_call(
        functools.partial(next_kernel, block=block, group=group, scale=scale),
        in_specs=[VMEM] * 4 + [pl.BlockSpec(memory_space=pl.ANY)],
        out_specs=VMEM,
        out_shape=jax.ShapeDtypeStruct((trials, 2 * cells), F32),
        scratch_shapes=scratch,
        compiler_params=pltpu.CompilerParams(vmem_limit_bytes=24 << 20),
        cost_estimate=pl.CostEstimate(flops=10**10, bytes_accessed=20 << 20, transcendentals=0),
        name="dedisperse_next",
    )(delays, table, turned, sums, order)


def wave_tables(side):
    angle = 2.0 * np.pi / side * np.arange(side)
    wave = np.repeat(np.stack([np.cos(angle), np.sin(angle)]), 8, axis=0).astype(np.float32)
    half = side // 2
    index = np.arange(half)[:, None] * np.arange(side)[None, :] % side
    cosine, sine = np.cos(angle)[index], np.sin(angle)[index]
    even = np.block([[cosine, cosine], [cosine, -cosine], [-sine, -sine], [-sine, sine]])
    odd = np.block([[cosine, cosine], [-sine, sine], [-sine, -sine], [-cosine, cosine]])
    stacked = []
    for matrix in (even, odd):
        high = matrix.astype(jnp.bfloat16)
        low = (matrix - high.astype(np.float64)).astype(jnp.bfloat16)
        stacked.append(np.concatenate([high, low], axis=0))
    return wave, np.stack(stacked)


def cell_kernel(u_ref, v_ref, wave_ref, order_ref, cos_ref, sin_ref, hot_ref, *, side):
    lanes = wave_ref.shape[1]
    u = u_ref[...]
    for r in range(0, side // 4, 8):
        row = lax.broadcasted_iota(jnp.int32, (8, lanes), 0) + r
        for c in range(0, u.shape[1], lanes):
            index = row * u[:, c : c + lanes] % side
            cos_ref[r : r + 8, c : c + lanes] = jnp.take_along_axis(wave_ref[0:8, :], index, axis=1)
            sin_ref[r : r + 8, c : c + lanes] = jnp.take_along_axis(wave_ref[8:16, :], index, axis=1)
    code = (u & 3) * (side // 2) + v_ref[...]
    rows = lax.broadcasted_iota(jnp.int32, (2 * side, u.shape[1]), 0)
    hot_ref[...] = jnp.where(rows == code, 1.0, 0.0).T.astype(BF16)


def split(value):
    high = value.astype(BF16)
    return high, (value - high.astype(F32)).astype(BF16)


def image_kernel(slot_ref, cos_ref, sin_ref, hot_ref, last_ref, *refs, side, weight, batch):
    pieces, refs = refs[:-10], refs[-10:]
    image_hbm, snr_ref, real_ref, imag_ref, peak_ref, power_ref, image_ref, sem, lefts, mids = refs
    trials, cells = pieces[0].shape[0], pieces[0].shape[1] // 2
    total = real_ref.shape[2]
    quarter = side // 4
    for b, piece in enumerate(pieces):
        lanes = pl.ds(pl.multiple_of((slot_ref[0] ^ b) * cells, cells), cells)
        value = (piece[...] * weight).reshape(trials // batch, batch, 2 * cells)
        real_ref[:, :, lanes] = value[:, :, :cells]
        imag_ref[:, :, lanes] = value[:, :, cells:]

    def image_copy(step):
        rows = pl.ds(step * batch, batch)
        return pltpu.make_async_copy(image_ref.at[rows], image_hbm.at[rows], sem.at[step])

    def load(step):
        for i in range(batch):
            real, imag = real_ref[step, i : i + 1, :], imag_ref[step, i : i + 1, :]
            cosine, sine = cos_ref[...], sin_ref[...]
            for part, value in enumerate((real * cosine - imag * sine, real * sine + imag * cosine)):
                rows = slice((2 * i + part) * quarter, (2 * i + part + 1) * quarter)
                high, low = split(value)
                lefts[step % 2, rows, :total] = high
                lefts[step % 2, rows, total:] = low

    def gather(step):
        left = lefts.at[step % 2]
        sums = jnp.dot(left[:, :total], hot_ref[...], preferred_element_type=F32)
        sums = sums + jnp.dot(left[:, total:], hot_ref[...], preferred_element_type=F32)
        first, second = sums[:, :side], sums[:, side:]
        for which, value in enumerate((first + second, first - second)):
            value = value.reshape(batch, 2, quarter, side)
            value = jnp.concatenate([value[:, 0], value[:, 1]], axis=2).reshape(batch * quarter, 2 * side)
            high, low = split(value)
            mids[step % 2, which, 0] = high
            mids[step % 2, which, 1] = low

    def turn(step):
        found = []
        for which in range(2):
            high, low = mids[step % 2, which, 0], mids[step % 2, which, 1]
            image = jnp.dot(low, last_ref[which, : 2 * side], preferred_element_type=F32)
            image = image + jnp.dot(high, last_ref[which, 2 * side :], preferred_element_type=F32)
            found.append(image + jnp.dot(high, last_ref[which, : 2 * side], preferred_element_type=F32))
        for i in range(batch):
            peak, power = None, None
            for q in range(4):
                half = slice(side * (q // 2), side * (q // 2 + 1))
                tile = found[q % 2][i * quarter : (i + 1) * quarter, half]
                image_ref[step * batch + i, q * quarter : (q + 1) * quarter, :] = tile
                peak = tile if q == 0 else jnp.maximum(peak, tile)
                power = tile * tile if q == 0 else power + tile * tile
            peak_ref[step, i : i + 1, :] = jnp.max(peak, axis=0, keepdims=True)
            power_ref[step, i : i + 1, :] = jnp.sum(power, axis=0, keepdims=True)
        image_copy(step).start()

    steps = trials // batch
    for step in range(steps + 2):
        if step >= 2:
            turn(step - 2)
        if 1 <= step <= steps:
            gather(step - 1)
        if step < steps:
            load(step)
    peak = jnp.max(peak_ref[...].reshape(trials, side), axis=1, keepdims=True)
    power = jnp.sum(power_ref[...].reshape(trials, side), axis=1, keepdims=True) / (side * side)
    snr = peak / jnp.sqrt(power + 1e-06)
    corner = lax.broadcasted_iota(jnp.int32, (trials, trials), 0) == lax.broadcasted_iota(jnp.int32, (trials, trials), 1)
    snr_ref[...] = jnp.sum(jnp.where(corner, snr, 0.0), axis=0, keepdims=True)
    for step in range(trials // batch):
        image_copy(step).wait()


def cell_tables(coord_u, coord_v, order, side):
    total = coord_u.shape[0]
    wave, _ = wave_tables(side)
    return pl.pallas_call(
        functools.partial(cell_kernel, side=side),
        in_specs=[VMEM] * 3 + [pl.BlockSpec(memory_space=pl.ANY)],
        out_specs=[VMEM] * 3,
        out_shape=[jax.ShapeDtypeStruct((side // 4, total), F32)] * 2 + [jax.ShapeDtypeStruct((total, 2 * side), BF16)],
        compiler_params=pltpu.CompilerParams(vmem_limit_bytes=16 << 20),
        cost_estimate=pl.CostEstimate(flops=10**9, bytes_accessed=1 << 20, transcendentals=0),
        name="cell_tables",
    )(coord_u.reshape(1, total), coord_v.reshape(1, total), jnp.asarray(wave), order)


def picture(pieces, slot, cells, side, weight):
    trials = pieces[0].shape[0]
    total = cells[0].shape[1]
    batch = math.gcd(8, trials)
    _, last = wave_tables(side)
    images, snr = pl.pallas_call(
        functools.partial(image_kernel, side=side, weight=weight, batch=batch),
        in_specs=[pl.BlockSpec(memory_space=pltpu.SMEM)] + [VMEM] * (4 + len(pieces)),
        out_specs=[pl.BlockSpec(memory_space=pltpu.HBM), VMEM],
        out_shape=[jax.ShapeDtypeStruct((trials, side, side), F32), jax.ShapeDtypeStruct((1, trials), F32)],
        scratch_shapes=[pltpu.VMEM((trials // batch, batch, total), F32)] * 2
        + [pltpu.VMEM((trials // batch, batch, side), F32)] * 2
        + [
            pltpu.VMEM((trials, side, side), F32),
            pltpu.SemaphoreType.DMA((trials // batch,)),
            pltpu.VMEM((2, batch * side // 2, 2 * total), BF16),
            pltpu.VMEM((2, 2, 2, batch * side // 4, 2 * side), BF16),
        ],
        compiler_params=pltpu.CompilerParams(vmem_limit_bytes=32 << 20),
        name="picture",
    )(slot.reshape(1), *cells, jnp.asarray(last), *pieces)
    return images, snr.reshape(trials)


def swap(value, axes, size, step):
    return lax.ppermute(value, axes, [(i, i ^ step) for i in range(size)])


def shards(visibilities, flags, delays, coord_u, coord_v, *, sizes):
    channels, times = visibilities.shape[1:3]
    trials, total_channels = delays.shape
    near = sizes["pol"] * sizes["sub"]
    own = trials // sizes["uv"]
    position = lax.axis_index("uv")
    slot = lax.axis_index(("pol", "sub"))
    scale = 1.0 / math.sqrt(total_channels * times)
    weight = 2.0 / math.sqrt(coord_u.shape[0])
    if own % 128 or channels % 128:
        rows = lax.dynamic_slice_in_dim(delays, position * channels, channels, 1)
        part = dedisperse_first(flags, rows, visibilities, scale, 1)[0]
        width = part.shape[1]
        part = part.reshape(sizes["uv"] * near, -1, width)
        held = lax.all_to_all(part, AXES, split_axis=0, concat_axis=0, tiled=True)
        held = held.reshape(sizes["uv"], near, -1, width).sum(axis=0)
        pieces = [lax.dynamic_index_in_dim(held, slot ^ i, 0, keepdims=False) for i in range(near)]
        return picture(pieces, slot, cell_tables(coord_u, coord_v, part, IMG), IMG, weight)

    last = sizes["uv"] - 1
    part, turned, sums, table, *rows = dedisperse_first(flags, delays, visibilities, scale, sizes["uv"])
    held = [swap(part, "uv", sizes["uv"], last)]
    for step in range(last - 1, -1, -1):
        part = dedisperse_next(rows[step], table, turned, sums, part, scale)
        if step:
            held.append(swap(part, "uv", sizes["uv"], step))
    for other in held:
        part = part + other
    cells = cell_tables(coord_u, coord_v, part, IMG)
    part = part.reshape(near, own // near, part.shape[1])
    pieces = [lax.dynamic_index_in_dim(part, slot ^ i, 0, keepdims=False) for i in range(near)]
    pieces = [pieces[0]] + [swap(pieces[i], ("pol", "sub"), near, i) for i in range(1, near)]
    return picture(pieces, slot, cells, IMG, weight)


def solution(mesh):
    in_specs = (P(None, "uv", "groups", ("pol", "sub")), P(("groups", "uv")), P(), P(), P())
    out_specs = (P(("groups", "uv", "pol", "sub"), None, None), P(("groups", "uv", "pol", "sub")))
    body = functools.partial(shards, sizes=dict(mesh.shape))
    return jax.shard_map(body, mesh=mesh, in_specs=in_specs, out_specs=out_specs, check_vma=False)
```

```python
import functools
import math

import jax
import jax.numpy as jnp
import numpy as np
from jax import lax
from jax.experimental import pallas as pl
from jax.experimental.pallas import tpu as pltpu
from jax.sharding import PartitionSpec as P

IMG = 128
FRAC = 8
AXES = ("uv", "pol", "sub")
F32 = jnp.float32
BF16 = jnp.bfloat16


def time_tables(times):
    t = np.arange(times)
    cot = np.where(t == 0, 2.0**60, 1.0 / np.tan(np.pi * np.where(t == 0, 1, t) / times))
    cot[times // 2] = 0.0
    cot = cot.astype(np.float32).astype(np.float64)
    power = 2.0 ** np.floor(16 - np.log2(np.maximum(np.abs(cot), 2.0**-10)))
    shifted = cot * power - np.where(t % 2 == 0, 1.0, -1.0) / times
    folded = np.minimum(t, times // 2)
    rows = [np.sin(np.pi * folded / times), np.cos(np.pi * folded / times), power, shifted]
    table = np.repeat(np.stack(rows), 8, axis=0)
    column = np.repeat(cot[:, None], times, axis=1)
    return np.concatenate([table, column]).astype(np.float32)


def coefficients(n, table_ref, times):
    cycle = FRAC * times
    height, width = n.shape
    lanes = table_ref.shape[1]
    fold = jnp.minimum(n, cycle - n)
    parts = []
    for i in range(4):
        index = (fold if i < 2 else n) >> 3
        source = table_ref[i * 8 : (i + 1) * 8, :]
        tiles = [
            [jnp.take_along_axis(source, index[r : r + 8, c : c + lanes], axis=1) for c in range(0, width, lanes)]
            for r in range(0, height, 8)
        ]
        parts.append(jnp.concatenate([jnp.concatenate(row, axis=1) for row in tiles], axis=0))
    sin_q, cos_q, power, shifted = parts
    theta = (fold & (FRAC - 1)).astype(F32) * (math.pi / cycle)
    square = theta * theta
    cos_r = 1.0 - square * (0.5 - square * (1.0 / 24.0))
    sin_r = theta * (1.0 - square * (1.0 / 6.0 - square * (1.0 / 120.0)))
    sin_a = sin_q * cos_r + cos_q * sin_r
    cos_a = cos_q * cos_r - sin_q * sin_r
    cos_a = jnp.where(n + n > cycle, -cos_a, cos_a)
    r = n & (FRAC - 1)
    side = jnp.abs(r - FRAC // 2)
    size = [math.cos(math.pi * i / FRAC) for i in range(FRAC // 2)]
    s = jnp.where(side == 0, size[0], jnp.where(side == 1, size[1], jnp.where(side == 2, size[2], size[3])))
    s = jnp.where((n & FRAC) == 0, s, -s)
    whole = r == 0
    ratio = sin_a / s
    u = jnp.where(whole, power, sin_a * ratio)
    w = jnp.where(whole, shifted, cos_a * ratio)
    k = jnp.where(whole, 0.0, s * cos_a / jnp.where(whole, 1.0, sin_a))
    return u, w, k, jnp.where(whole, 0.0, s)


def prepare(delays_ref, const_ref, u_ref, w_ref, k_ref, channels, times):
    trials = delays_ref.shape[2]
    many = math.gcd(16, channels // 8)

    def body(i, carry):
        rows = pl.ds(i * many, many)
        n = delays_ref[rows].reshape(many * 8, trials)
        u, w, k, s = coefficients(n, const_ref, times)
        u_ref[rows] = u.reshape(many, 8, trials)
        w_ref[rows] = w.reshape(many, 8, trials)
        size = many * 8
        k_ref[pl.ds(pl.multiple_of(i * size, 8), size), :] = k
        k_ref[pl.ds(pl.multiple_of(channels + i * size, 8), size), :] = s
        return carry

    lax.fori_loop(0, channels // 8 // many, body, 0)


def fill(right, u, w, const_ref, start, times):
    tiles = len(right) // 2
    for b in range(tiles):
        lanes = slice(b * 128, (b + 1) * 128)
        for t in range(0, times, 16):
            bottom = const_ref[32 + t : 48 + t, :] * u[:, lanes] - w[:, lanes]
            guess = pltpu.reciprocal(bottom, approx=True)
            high = guess.astype(BF16)
            rest = (1.0 - bottom * high.astype(F32)).astype(BF16) * high
            right[b][start + t : start + t + 16, :] = high
            right[tiles + b][start + t : start + t + 16, :] = rest


def join(refs):
    return jnp.concatenate([ref[...] for ref in refs], axis=1)


def finish(acc_ref, k_ref, sums, out_ref, trials, scale):
    cells = sums.shape[1] // 2
    real, imag = sums[:, :cells], sums[:, cells:]
    right = jnp.concatenate([sums, jnp.concatenate([imag, -real], axis=1)], axis=0)
    extra = jnp.dot(k_ref[...].T, right, precision=lax.Precision.HIGHEST, preferred_element_type=F32)
    main = (acc_ref[:, :trials] + acc_ref[:, trials:]).T
    out_ref[...] = (main + extra) * scale


def first_kernel(
    flags_hbm, const_hbm, delays_hbm, vis_hbm, out_ref, turned_ref, sums_ref, const_ref, *refs,
    block, group, copies, scale, blocks,
):
    _, channels, times, cells = vis_hbm.shape
    total, trials = delays_hbm.shape[0], out_ref.shape[0]
    later = [refs[i] for i in range(blocks - 1)]
    vis_ref, delays_ref, flags_ref, sem, side, first_ref, pick_ref = refs[blocks - 1 : blocks + 6]
    acc_ref, u_ref, w_ref, k_ref = refs[blocks + 6 : blocks + 10]
    pairs = refs[blocks + 10 :]
    tiles = 2 * (trials // 128)
    per = channels // copies
    at = lax.axis_index("uv") if blocks > 1 else 0
    lanes = pl.ds(pl.multiple_of(at * channels, channels), channels) if blocks > 1 else slice(None)
    small = [
        pltpu.make_async_copy(delays_hbm.at[:, lanes], delays_ref, side.at[0]),
        pltpu.make_async_copy(const_hbm, const_ref, side.at[1]),
        pltpu.make_async_copy(flags_hbm, flags_ref, side.at[2]),
    ]
    for copy in small:
        copy.start()

    def sample_copy(i, p):
        rows = pl.ds(i * per, per)
        return pltpu.make_async_copy(vis_hbm.at[p, rows], vis_ref.at[p, rows], sem.at[p, i])

    for i in range(copies):
        for p in range(2):
            sample_copy(i, p).start()
    acc_ref[...] = jnp.zeros_like(acc_ref)
    for copy in small:
        copy.wait()
    for step in range(blocks):
        mine = pl.ds(pl.multiple_of((at ^ step) * trials, trials), trials) if blocks > 1 else slice(None)
        turned = delays_ref[mine, :].T.reshape(channels // 8, 8, trials)
        (later[step] if step < blocks - 1 else first_ref)[...] = turned
    prepare(first_ref, const_ref, u_ref, w_ref, k_ref, channels, times)
    odd = lax.broadcasted_iota(jnp.int32, (1, times), 1) % 2
    sign_row = jnp.where(odd == 0, 1.0, -1.0)
    height = pick_ref.shape[1]
    pick = lax.broadcasted_iota(jnp.int32, (height, times), 0)
    wide_sign = jnp.broadcast_to(sign_row, (height, times))
    for at in range(block):
        lanes = slice(at % group * times, (at % group + 1) * times)
        pick_ref[at // group, :, lanes] = jnp.where(pick == at, wide_sign, 0.0).astype(BF16)

    def body(step, carry):
        total = None
        rows_sum = None
        waits = block // per
        for i in range(block // group):
            if i * group % per == 0:
                for p in range(2):
                    sample_copy(step * waits + i * group // per, p).wait()
            right = pairs[i * tiles : (i + 1) * tiles]
            for j in range(group):
                at = i * group + j
                c = step * block + at
                row = step * (block // 8) + at // 8
                one = slice(at % 8, at % 8 + 1)
                signs = (sign_row * flags_ref[c].astype(F32)).astype(BF16)
                for p in range(2):
                    turned = vis_ref[p, c].T * signs
                    turned_ref[c, p * cells : (p + 1) * cells, :] = turned
                fill(right, u_ref[row, one, :], w_ref[row, one, :], const_ref, j * times, times)
            left = jnp.concatenate([turned_ref[step * block + i * group + j] for j in range(group)], axis=1)
            product = jnp.dot(left, join(right), preferred_element_type=F32)
            total = product if total is None else total + product
            here = pl.ds(step * block + i * group, group)
            natural = [vis_ref[p, here].reshape(group * times, cells) for p in range(2)]
            product = jnp.dot(pick_ref[i], jnp.concatenate(natural, axis=1), preferred_element_type=F32)
            rows_sum = product if rows_sum is None else rows_sum + product
        acc_ref[...] += total
        for at in range(block):
            keep = flags_ref[step * block + at].astype(F32)
            sums_ref[step * (block // 8) + at // 8, at % 8 : at % 8 + 1, :] = rows_sum[at : at + 1, :] * keep
        return carry

    lax.fori_loop(0, channels // block, body, 0)
    finish(acc_ref, k_ref, sums_ref[...].reshape(channels, 2 * cells), out_ref, trials, scale)


def next_kernel(
    delays_ref, const_ref, turned_ref, sums_ref, order_ref, out_ref,
    acc_ref, u_ref, w_ref, k_ref, *pairs, block, group, scale,
):
    channels, _, times = turned_ref.shape
    trials = delays_ref.shape[2]
    tiles = 2 * (trials // 128)
    prepare(delays_ref, const_ref, u_ref, w_ref, k_ref, channels, times)
    acc_ref[...] = jnp.zeros_like(acc_ref)

    def body(step, carry):
        total = None
        for i in range(block // group):
            right = pairs[i * tiles : (i + 1) * tiles]
            for j in range(group):
                at = i * group + j
                row = step * (block // 8) + at // 8
                one = slice(at % 8, at % 8 + 1)
                fill(right, u_ref[row, one, :], w_ref[row, one, :], const_ref, j * times, times)
            left = jnp.concatenate([turned_ref[step * block + i * group + j] for j in range(group)], axis=1)
            product = jnp.dot(left, join(right), preferred_element_type=F32)
            total = product if total is None else total + product
        acc_ref[...] += total
        return carry

    lax.fori_loop(0, channels // block, body, 0)
    finish(acc_ref, k_ref, sums_ref[...].reshape(channels, sums_ref.shape[2]), out_ref, trials, scale)


def working(trials, channels, cells):
    return [
        pltpu.VMEM((2 * cells, 2 * trials), F32),
        pltpu.VMEM((channels // 8, 8, trials), F32),
        pltpu.VMEM((channels // 8, 8, trials), F32),
        pltpu.VMEM((2 * channels, trials), F32),
    ]


VMEM = pl.BlockSpec(memory_space=pltpu.VMEM)


def dedisperse_first(flags, delays, visibilities, scale, blocks):
    _, channels, times, cells = visibilities.shape
    trials = delays.shape[0] // blocks
    block, group = math.gcd(64, channels), 2
    copies = channels // block
    table = time_tables(times)
    turned_delays = (channels // 8, 8, trials)
    scratch = [
        pltpu.VMEM(visibilities.shape, visibilities.dtype),
        pltpu.VMEM((delays.shape[0], channels), jnp.int32),
        pltpu.SMEM((channels,), jnp.int32),
        pltpu.SemaphoreType.DMA((2, copies)),
        pltpu.SemaphoreType.DMA((3,)),
        pltpu.VMEM(turned_delays, jnp.int32),
        pltpu.VMEM((block // group, max(16, block), group * times), BF16),
    ]
    scratch += working(trials, channels, cells)
    for _ in range(block // group):
        scratch += [pltpu.VMEM((group * times, 128), BF16)] * (2 * (trials // 128))
    hbm = pl.BlockSpec(memory_space=pltpu.HBM)
    return pl.pallas_call(
        functools.partial(first_kernel, block=block, group=group, copies=copies, scale=scale, blocks=blocks),
        in_specs=[hbm] * 4,
        out_specs=[VMEM] * (3 + blocks),
        out_shape=[
            jax.ShapeDtypeStruct((trials, 2 * cells), F32),
            jax.ShapeDtypeStruct((channels, 2 * cells, times), BF16),
            jax.ShapeDtypeStruct((channels // 8, 8, 2 * cells), F32),
            jax.ShapeDtypeStruct(table.shape, F32),
        ] + [jax.ShapeDtypeStruct(turned_delays, jnp.int32)] * (blocks - 1),
        scratch_shapes=scratch,
        compiler_params=pltpu.CompilerParams(vmem_limit_bytes=32 << 20),
        cost_estimate=pl.CostEstimate(flops=10**10, bytes_accessed=20 << 20, transcendentals=0),
        name="dedisperse_first",
    )(*[pltpu.with_memory_space_constraint(x, pltpu.HBM) for x in (flags, jnp.asarray(table), delays, visibilities)])


def dedisperse_next(delays, table, turned, sums, order, scale):
    channels, cells, times = turned.shape
    cells //= 2
    trials = delays.shape[2]
    block, group = math.gcd(128, channels), 2
    scratch = working(trials, channels, cells)
    scratch += [pltpu.VMEM((group * times, 128), BF16)] * (2 * (trials // 128) * (block // group))
    return pl.pallas_call(
        functools.partial(next_kernel, block=block, group=group, scale=scale),
        in_specs=[VMEM] * 4 + [pl.BlockSpec(memory_space=pl.ANY)],
        out_specs=VMEM,
        out_shape=jax.ShapeDtypeStruct((trials, 2 * cells), F32),
        scratch_shapes=scratch,
        compiler_params=pltpu.CompilerParams(vmem_limit_bytes=24 << 20),
        cost_estimate=pl.CostEstimate(flops=10**10, bytes_accessed=20 << 20, transcendentals=0),
        name="dedisperse_next",
    )(delays, table, turned, sums, order)


def wave_tables(side):
    angle = 2.0 * np.pi / side * np.arange(side)
    wave = np.repeat(np.stack([np.cos(angle), np.sin(angle)]), 8, axis=0).astype(np.float32)
    half = side // 2
    index = np.arange(half)[:, None] * np.arange(side)[None, :] % side
    cosine, sine = np.cos(angle)[index], np.sin(angle)[index]
    even = np.block([[cosine, cosine], [cosine, -cosine], [-sine, -sine], [-sine, sine]])
    odd = np.block([[cosine, cosine], [-sine, sine], [-sine, -sine], [-cosine, cosine]])
    stacked = []
    for matrix in (even, odd):
        high = matrix.astype(jnp.bfloat16)
        low = (matrix - high.astype(np.float64)).astype(jnp.bfloat16)
        stacked.append(np.concatenate([high, low], axis=0))
    return wave, np.stack(stacked)


def cell_kernel(u_ref, v_ref, wave_ref, order_ref, cos_ref, sin_ref, hot_ref, *, side):
    lanes = wave_ref.shape[1]
    u = u_ref[...]
    for r in range(0, side // 4, 8):
        row = lax.broadcasted_iota(jnp.int32, (8, lanes), 0) + r
        for c in range(0, u.shape[1], lanes):
            index = row * u[:, c : c + lanes] % side
            cos_ref[r : r + 8, c : c + lanes] = jnp.take_along_axis(wave_ref[0:8, :], index, axis=1)
            sin_ref[r : r + 8, c : c + lanes] = jnp.take_along_axis(wave_ref[8:16, :], index, axis=1)
    code = (u & 3) * (side // 2) + v_ref[...]
    rows = lax.broadcasted_iota(jnp.int32, (2 * side, u.shape[1]), 0)
    hot_ref[...] = jnp.where(rows == code, 1.0, 0.0).T.astype(BF16)


def split(value):
    high = value.astype(BF16)
    return high, (value - high.astype(F32)).astype(BF16)


def image_kernel(slot_ref, cos_ref, sin_ref, hot_ref, last_ref, *refs, side, weight, batch):
    pieces, refs = refs[:-10], refs[-10:]
    image_hbm, snr_ref, real_ref, imag_ref, peak_ref, power_ref, image_ref, sem, lefts, mids = refs
    trials, cells = pieces[0].shape[0], pieces[0].shape[1] // 2
    total = real_ref.shape[2]
    quarter = side // 4
    for b, piece in enumerate(pieces):
        lanes = pl.ds(pl.multiple_of((slot_ref[0] ^ b) * cells, cells), cells)
        value = (piece[...] * weight).reshape(trials // batch, batch, 2 * cells)
        real_ref[:, :, lanes] = value[:, :, :cells]
        imag_ref[:, :, lanes] = value[:, :, cells:]

    def image_copy(step):
        rows = pl.ds(step * batch, batch)
        return pltpu.make_async_copy(image_ref.at[rows], image_hbm.at[rows], sem.at[step])

    def load(step):
        for i in range(batch):
            real, imag = real_ref[step, i : i + 1, :], imag_ref[step, i : i + 1, :]
            cosine, sine = cos_ref[...], sin_ref[...]
            for part, value in enumerate((real * cosine - imag * sine, real * sine + imag * cosine)):
                rows = slice((2 * i + part) * quarter, (2 * i + part + 1) * quarter)
                high, low = split(value)
                lefts[step % 2, rows, :total] = high
                lefts[step % 2, rows, total:] = low

    def gather(step):
        left = lefts.at[step % 2]
        sums = jnp.dot(left[:, :total], hot_ref[...], preferred_element_type=F32)
        sums = sums + jnp.dot(left[:, total:], hot_ref[...], preferred_element_type=F32)
        first, second = sums[:, :side], sums[:, side:]
        for which, value in enumerate((first + second, first - second)):
            value = value.reshape(batch, 2, quarter, side)
            value = jnp.concatenate([value[:, 0], value[:, 1]], axis=2).reshape(batch * quarter, 2 * side)
            high, low = split(value)
            mids[step % 2, which, 0] = high
            mids[step % 2, which, 1] = low

    def turn(step):
        found = []
        for which in range(2):
            high, low = mids[step % 2, which, 0], mids[step % 2, which, 1]
            image = jnp.dot(low, last_ref[which, : 2 * side], preferred_element_type=F32)
            image = image + jnp.dot(high, last_ref[which, 2 * side :], preferred_element_type=F32)
            found.append(image + jnp.dot(high, last_ref[which, : 2 * side], preferred_element_type=F32))
        for i in range(batch):
            peak, power = None, None
            for q in range(4):
                half = slice(side * (q // 2), side * (q // 2 + 1))
                tile = found[q % 2][i * quarter : (i + 1) * quarter, half]
                image_ref[step * batch + i, q * quarter : (q + 1) * quarter, :] = tile
                peak = tile if q == 0 else jnp.maximum(peak, tile)
                power = tile * tile if q == 0 else power + tile * tile
            peak_ref[step, i : i + 1, :] = jnp.max(peak, axis=0, keepdims=True)
            power_ref[step, i : i + 1, :] = jnp.sum(power, axis=0, keepdims=True)
        image_copy(step).start()

    steps = trials // batch
    for step in range(steps + 2):
        if step >= 2:
            turn(step - 2)
        if 1 <= step <= steps:
            gather(step - 1)
        if step < steps:
            load(step)
    peak = jnp.max(peak_ref[...].reshape(trials, side), axis=1, keepdims=True)
    power = jnp.sum(power_ref[...].reshape(trials, side), axis=1, keepdims=True) / (side * side)
    snr = peak / jnp.sqrt(power + 1e-06)
    corner = lax.broadcasted_iota(jnp.int32, (trials, trials), 0) == lax.broadcasted_iota(jnp.int32, (trials, trials), 1)
    snr_ref[...] = jnp.sum(jnp.where(corner, snr, 0.0), axis=0, keepdims=True)
    for step in range(trials // batch):
        image_copy(step).wait()


def cell_tables(coord_u, coord_v, order, side):
    total = coord_u.shape[0]
    wave, _ = wave_tables(side)
    return pl.pallas_call(
        functools.partial(cell_kernel, side=side),
        in_specs=[VMEM] * 3 + [pl.BlockSpec(memory_space=pl.ANY)],
        out_specs=[VMEM] * 3,
        out_shape=[jax.ShapeDtypeStruct((side // 4, total), F32)] * 2 + [jax.ShapeDtypeStruct((total, 2 * side), BF16)],
        compiler_params=pltpu.CompilerParams(vmem_limit_bytes=16 << 20),
        cost_estimate=pl.CostEstimate(flops=10**9, bytes_accessed=1 << 20, transcendentals=0),
        name="cell_tables",
    )(coord_u.reshape(1, total), coord_v.reshape(1, total), jnp.asarray(wave), order)


def picture(pieces, slot, cells, side, weight):
    trials = pieces[0].shape[0]
    total = cells[0].shape[1]
    batch = math.gcd(8, trials)
    _, last = wave_tables(side)
    images, snr = pl.pallas_call(
        functools.partial(image_kernel, side=side, weight=weight, batch=batch),
        in_specs=[pl.BlockSpec(memory_space=pltpu.SMEM)] + [VMEM] * (4 + len(pieces)),
        out_specs=[pl.BlockSpec(memory_space=pltpu.HBM), VMEM],
        out_shape=[jax.ShapeDtypeStruct((trials, side, side), F32), jax.ShapeDtypeStruct((1, trials), F32)],
        scratch_shapes=[pltpu.VMEM((trials // batch, batch, total), F32)] * 2
        + [pltpu.VMEM((trials // batch, batch, side), F32)] * 2
        + [
            pltpu.VMEM((trials, side, side), F32),
            pltpu.SemaphoreType.DMA((trials // batch,)),
            pltpu.VMEM((2, batch * side // 2, 2 * total), BF16),
            pltpu.VMEM((2, 2, 2, batch * side // 4, 2 * side), BF16),
        ],
        compiler_params=pltpu.CompilerParams(vmem_limit_bytes=32 << 20),
        name="picture",
    )(slot.reshape(1), *cells, jnp.asarray(last), *pieces)
    return images, snr.reshape(trials)


def swap(value, axes, size, step):
    return lax.ppermute(value, axes, [(i, i ^ step) for i in range(size)])


def shards(visibilities, flags, delays, coord_u, coord_v, *, sizes):
    channels, times = visibilities.shape[1:3]
    trials, total_channels = delays.shape
    near = sizes["pol"] * sizes["sub"]
    own = trials // sizes["uv"]
    position = lax.axis_index("uv")
    slot = lax.axis_index(("pol", "sub"))
    scale = 1.0 / math.sqrt(total_channels * times)
    weight = 2.0 / math.sqrt(coord_u.shape[0])
    if own % 128 or channels % 128:
        rows = lax.dynamic_slice_in_dim(delays, position * channels, channels, 1)
        part = dedisperse_first(flags, rows, visibilities, scale, 1)[0]
        width = part.shape[1]
        part = part.reshape(sizes["uv"] * near, -1, width)
        held = lax.all_to_all(part, AXES, split_axis=0, concat_axis=0, tiled=True)
        held = held.reshape(sizes["uv"], near, -1, width).sum(axis=0)
        pieces = [lax.dynamic_index_in_dim(held, slot ^ i, 0, keepdims=False) for i in range(near)]
        return picture(pieces, slot, cell_tables(coord_u, coord_v, part, IMG), IMG, weight)

    last = sizes["uv"] - 1
    part, turned, sums, table, *rows = dedisperse_first(flags, delays, visibilities, scale, sizes["uv"])
    held = [swap(part, "uv", sizes["uv"], last)]
    for step in range(last - 1, -1, -1):
        part = dedisperse_next(rows[step], table, turned, sums, part, scale)
        if step:
            held.append(swap(part, "uv", sizes["uv"], step))
    for other in held:
        part = part + other
    cells = cell_tables(coord_u, coord_v, part, IMG)
    part = part.reshape(near, own // near, part.shape[1])
    pieces = [lax.dynamic_index_in_dim(part, slot ^ i, 0, keepdims=False) for i in range(near)]
    for i in range(near - 1, 0, -1):
        pieces[i] = swap(pieces[i], ("pol", "sub"), near, i)
    return picture(pieces, slot, cells, IMG, weight)


def solution(mesh):
    in_specs = (P(None, "uv", "groups", ("pol", "sub")), P(("groups", "uv")), P(), P(), P())
    out_specs = (P(("groups", "uv", "pol", "sub"), None, None), P(("groups", "uv", "pol", "sub")))
    body = functools.partial(shards, sizes=dict(mesh.shape))
    return jax.shard_map(body, mesh=mesh, in_specs=in_specs, out_specs=out_specs, check_vma=False)
```

```python
import functools
import math

import jax
import jax.numpy as jnp
import numpy as np
from jax import lax
from jax.experimental import pallas as pl
from jax.experimental.pallas import tpu as pltpu
from jax.sharding import PartitionSpec as P

IMG = 128
FRAC = 8
AXES = ("uv", "pol", "sub")
F32 = jnp.float32
BF16 = jnp.bfloat16


def time_tables(times):
    t = np.arange(times)
    cot = np.where(t == 0, 2.0**60, 1.0 / np.tan(np.pi * np.where(t == 0, 1, t) / times))
    cot[times // 2] = 0.0
    cot = cot.astype(np.float32).astype(np.float64)
    power = 2.0 ** np.floor(16 - np.log2(np.maximum(np.abs(cot), 2.0**-10)))
    shifted = cot * power - np.where(t % 2 == 0, 1.0, -1.0) / times
    folded = np.minimum(t, times // 2)
    rows = [np.sin(np.pi * folded / times), np.cos(np.pi * folded / times), power, shifted]
    table = np.repeat(np.stack(rows), 8, axis=0)
    column = np.repeat(cot[:, None], times, axis=1)
    return np.concatenate([table, column]).astype(np.float32)


def coefficients(n, table_ref, times):
    cycle = FRAC * times
    height, width = n.shape
    lanes = table_ref.shape[1]
    fold = jnp.minimum(n, cycle - n)
    parts = []
    for i in range(4):
        index = (fold if i < 2 else n) >> 3
        source = table_ref[i * 8 : (i + 1) * 8, :]
        tiles = [
            [jnp.take_along_axis(source, index[r : r + 8, c : c + lanes], axis=1) for c in range(0, width, lanes)]
            for r in range(0, height, 8)
        ]
        parts.append(jnp.concatenate([jnp.concatenate(row, axis=1) for row in tiles], axis=0))
    sin_q, cos_q, power, shifted = parts
    theta = (fold & (FRAC - 1)).astype(F32) * (math.pi / cycle)
    square = theta * theta
    cos_r = 1.0 - square * (0.5 - square * (1.0 / 24.0))
    sin_r = theta * (1.0 - square * (1.0 / 6.0 - square * (1.0 / 120.0)))
    sin_a = sin_q * cos_r + cos_q * sin_r
    cos_a = cos_q * cos_r - sin_q * sin_r
    cos_a = jnp.where(n + n > cycle, -cos_a, cos_a)
    r = n & (FRAC - 1)
    side = jnp.abs(r - FRAC // 2)
    size = [math.cos(math.pi * i / FRAC) for i in range(FRAC // 2)]
    s = jnp.where(side == 0, size[0], jnp.where(side == 1, size[1], jnp.where(side == 2, size[2], size[3])))
    s = jnp.where((n & FRAC) == 0, s, -s)
    whole = r == 0
    ratio = sin_a / s
    u = jnp.where(whole, power, sin_a * ratio)
    w = jnp.where(whole, shifted, cos_a * ratio)
    k = jnp.where(whole, 0.0, s * cos_a / jnp.where(whole, 1.0, sin_a))
    return u, w, k, jnp.where(whole, 0.0, s)


def prepare(delays_ref, const_ref, u_ref, w_ref, k_ref, channels, times):
    trials = delays_ref.shape[2]
    many = math.gcd(16, channels // 8)

    def body(i, carry):
        rows = pl.ds(i * many, many)
        n = delays_ref[rows].reshape(many * 8, trials)
        u, w, k, s = coefficients(n, const_ref, times)
        u_ref[rows] = u.reshape(many, 8, trials)
        w_ref[rows] = w.reshape(many, 8, trials)
        size = many * 8
        k_ref[pl.ds(pl.multiple_of(i * size, 8), size), :] = k
        k_ref[pl.ds(pl.multiple_of(channels + i * size, 8), size), :] = s
        return carry

    lax.fori_loop(0, channels // 8 // many, body, 0)


def fill(right, u, w, const_ref, start, times):
    tiles = len(right) // 2
    for b in range(tiles):
        lanes = slice(b * 128, (b + 1) * 128)
        for t in range(0, times, 16):
            bottom = const_ref[32 + t : 48 + t, :] * u[:, lanes] - w[:, lanes]
            guess = pltpu.reciprocal(bottom, approx=True)
            high = guess.astype(BF16)
            rest = (1.0 - bottom * high.astype(F32)).astype(BF16) * high
            right[b][start + t : start + t + 16, :] = high
            right[tiles + b][start + t : start + t + 16, :] = rest


def join(refs):
    return jnp.concatenate([ref[...] for ref in refs], axis=1)


def finish(acc_ref, k_ref, sums, out_ref, trials, scale):
    cells = sums.shape[1] // 2
    real, imag = sums[:, :cells], sums[:, cells:]
    right = jnp.concatenate([sums, jnp.concatenate([imag, -real], axis=1)], axis=0)
    extra = jnp.dot(k_ref[...].T, right, precision=lax.Precision.HIGHEST, preferred_element_type=F32)
    main = (acc_ref[:, :trials] + acc_ref[:, trials:]).T
    out_ref[...] = (main + extra) * scale


def first_kernel(
    flags_hbm, const_hbm, delays_hbm, vis_hbm, out_ref, turned_ref, sums_ref, const_ref, *refs,
    block, group, copies, scale, blocks,
):
    _, channels, times, cells = vis_hbm.shape
    total, trials = delays_hbm.shape[0], out_ref.shape[0]
    later = [refs[i] for i in range(blocks - 1)]
    vis_ref, delays_ref, flags_ref, sem, side, first_ref, pick_ref = refs[blocks - 1 : blocks + 6]
    acc_ref, u_ref, w_ref, k_ref = refs[blocks + 6 : blocks + 10]
    pairs = refs[blocks + 10 :]
    tiles = 2 * (trials // 128)
    per = channels // copies
    at = lax.axis_index("uv") if blocks > 1 else 0
    lanes = pl.ds(pl.multiple_of(at * channels, channels), channels) if blocks > 1 else slice(None)
    small = [
        pltpu.make_async_copy(delays_hbm.at[:, lanes], delays_ref, side.at[0]),
        pltpu.make_async_copy(const_hbm, const_ref, side.at[1]),
        pltpu.make_async_copy(flags_hbm, flags_ref, side.at[2]),
    ]
    for copy in small:
        copy.start()

    def sample_copy(i, p):
        rows = pl.ds(i * per, per)
        return pltpu.make_async_copy(vis_hbm.at[p, rows], vis_ref.at[p, rows], sem.at[p, i])

    for i in range(copies):
        for p in range(2):
            sample_copy(i, p).start()
    acc_ref[...] = jnp.zeros_like(acc_ref)
    for copy in small:
        copy.wait()
    for step in range(blocks):
        mine = pl.ds(pl.multiple_of((at ^ step) * trials, trials), trials) if blocks > 1 else slice(None)
        turned = delays_ref[mine, :].T.reshape(channels // 8, 8, trials)
        (later[step] if step < blocks - 1 else first_ref)[...] = turned
    prepare(first_ref, const_ref, u_ref, w_ref, k_ref, channels, times)
    odd = lax.broadcasted_iota(jnp.int32, (1, times), 1) % 2
    sign_row = jnp.where(odd == 0, 1.0, -1.0)
    height = pick_ref.shape[1]
    pick = lax.broadcasted_iota(jnp.int32, (height, times), 0)
    wide_sign = jnp.broadcast_to(sign_row, (height, times))
    for at in range(block):
        lanes = slice(at % group * times, (at % group + 1) * times)
        pick_ref[at // group, :, lanes] = jnp.where(pick == at, wide_sign, 0.0).astype(BF16)

    def body(step, carry):
        total = None
        rows_sum = None
        waits = block // per
        for i in range(block // group):
            if i * group % per == 0:
                for p in range(2):
                    sample_copy(step * waits + i * group // per, p).wait()
            right = pairs[i * tiles : (i + 1) * tiles]
            for j in range(group):
                at = i * group + j
                c = step * block + at
                row = step * (block // 8) + at // 8
                one = slice(at % 8, at % 8 + 1)
                signs = (sign_row * flags_ref[c].astype(F32)).astype(BF16)
                for p in range(2):
                    turned = vis_ref[p, c].T * signs
                    turned_ref[c, p * cells : (p + 1) * cells, :] = turned
                fill(right, u_ref[row, one, :], w_ref[row, one, :], const_ref, j * times, times)
            left = jnp.concatenate([turned_ref[step * block + i * group + j] for j in range(group)], axis=1)
            product = jnp.dot(left, join(right), preferred_element_type=F32)
            total = product if total is None else total + product
            here = pl.ds(step * block + i * group, group)
            natural = [vis_ref[p, here].reshape(group * times, cells) for p in range(2)]
            product = jnp.dot(pick_ref[i], jnp.concatenate(natural, axis=1), preferred_element_type=F32)
            rows_sum = product if rows_sum is None else rows_sum + product
        acc_ref[...] += total
        for at in range(block):
            keep = flags_ref[step * block + at].astype(F32)
            sums_ref[step * (block // 8) + at // 8, at % 8 : at % 8 + 1, :] = rows_sum[at : at + 1, :] * keep
        return carry

    lax.fori_loop(0, channels // block, body, 0)
    finish(acc_ref, k_ref, sums_ref[...].reshape(channels, 2 * cells), out_ref, trials, scale)


def next_kernel(
    delays_ref, const_ref, turned_ref, sums_ref, order_ref, out_ref,
    acc_ref, u_ref, w_ref, k_ref, *pairs, block, group, scale,
):
    channels, _, times = turned_ref.shape
    trials = delays_ref.shape[2]
    tiles = 2 * (trials // 128)
    prepare(delays_ref, const_ref, u_ref, w_ref, k_ref, channels, times)
    acc_ref[...] = jnp.zeros_like(acc_ref)

    def body(step, carry):
        total = None
        for i in range(block // group):
            right = pairs[i * tiles : (i + 1) * tiles]
            for j in range(group):
                at = i * group + j
                row = step * (block // 8) + at // 8
                one = slice(at % 8, at % 8 + 1)
                fill(right, u_ref[row, one, :], w_ref[row, one, :], const_ref, j * times, times)
            left = jnp.concatenate([turned_ref[step * block + i * group + j] for j in range(group)], axis=1)
            product = jnp.dot(left, join(right), preferred_element_type=F32)
            total = product if total is None else total + product
        acc_ref[...] += total
        return carry

    lax.fori_loop(0, channels // block, body, 0)
    finish(acc_ref, k_ref, sums_ref[...].reshape(channels, sums_ref.shape[2]), out_ref, trials, scale)


def working(trials, channels, cells):
    return [
        pltpu.VMEM((2 * cells, 2 * trials), F32),
        pltpu.VMEM((channels // 8, 8, trials), F32),
        pltpu.VMEM((channels // 8, 8, trials), F32),
        pltpu.VMEM((2 * channels, trials), F32),
    ]


VMEM = pl.BlockSpec(memory_space=pltpu.VMEM)


def dedisperse_first(flags, delays, visibilities, scale, blocks):
    _, channels, times, cells = visibilities.shape
    trials = delays.shape[0] // blocks
    block, group = math.gcd(64, channels), 2
    copies = channels // block
    table = time_tables(times)
    turned_delays = (channels // 8, 8, trials)
    scratch = [
        pltpu.VMEM(visibilities.shape, visibilities.dtype),
        pltpu.VMEM((delays.shape[0], channels), jnp.int32),
        pltpu.SMEM((channels,), jnp.int32),
        pltpu.SemaphoreType.DMA((2, copies)),
        pltpu.SemaphoreType.DMA((3,)),
        pltpu.VMEM(turned_delays, jnp.int32),
        pltpu.VMEM((block // group, max(16, block), group * times), BF16),
    ]
    scratch += working(trials, channels, cells)
    for _ in range(block // group):
        scratch += [pltpu.VMEM((group * times, 128), BF16)] * (2 * (trials // 128))
    hbm = pl.BlockSpec(memory_space=pltpu.HBM)
    return pl.pallas_call(
        functools.partial(first_kernel, block=block, group=group, copies=copies, scale=scale, blocks=blocks),
        in_specs=[hbm] * 4,
        out_specs=[VMEM] * (3 + blocks),
        out_shape=[
            jax.ShapeDtypeStruct((trials, 2 * cells), F32),
            jax.ShapeDtypeStruct((channels, 2 * cells, times), BF16),
            jax.ShapeDtypeStruct((channels // 8, 8, 2 * cells), F32),
            jax.ShapeDtypeStruct(table.shape, F32),
        ] + [jax.ShapeDtypeStruct(turned_delays, jnp.int32)] * (blocks - 1),
        scratch_shapes=scratch,
        compiler_params=pltpu.CompilerParams(vmem_limit_bytes=32 << 20),
        cost_estimate=pl.CostEstimate(flops=10**10, bytes_accessed=20 << 20, transcendentals=0),
        name="dedisperse_first",
    )(*[pltpu.with_memory_space_constraint(x, pltpu.HBM) for x in (flags, jnp.asarray(table), delays, visibilities)])


def dedisperse_next(delays, table, turned, sums, order, scale):
    channels, cells, times = turned.shape
    cells //= 2
    trials = delays.shape[2]
    block, group = math.gcd(128, channels), 2
    scratch = working(trials, channels, cells)
    scratch += [pltpu.VMEM((group * times, 128), BF16)] * (2 * (trials // 128) * (block // group))
    return pl.pallas_call(
        functools.partial(next_kernel, block=block, group=group, scale=scale),
        in_specs=[VMEM] * 4 + [pl.BlockSpec(memory_space=pl.ANY)],
        out_specs=VMEM,
        out_shape=jax.ShapeDtypeStruct((trials, 2 * cells), F32),
        scratch_shapes=scratch,
        compiler_params=pltpu.CompilerParams(vmem_limit_bytes=24 << 20),
        cost_estimate=pl.CostEstimate(flops=10**10, bytes_accessed=20 << 20, transcendentals=0),
        name="dedisperse_next",
    )(delays, table, turned, sums, order)


def wave_tables(side):
    angle = 2.0 * np.pi / side * np.arange(side)
    wave = np.repeat(np.stack([np.cos(angle), np.sin(angle)]), 8, axis=0).astype(np.float32)
    half = side // 2
    index = np.arange(half)[:, None] * np.arange(side)[None, :] % side
    cosine, sine = np.cos(angle)[index], np.sin(angle)[index]
    even = np.block([[cosine, cosine], [cosine, -cosine], [-sine, -sine], [-sine, sine]])
    odd = np.block([[cosine, cosine], [-sine, sine], [-sine, -sine], [-cosine, cosine]])
    stacked = []
    for matrix in (even, odd):
        high = matrix.astype(jnp.bfloat16)
        low = (matrix - high.astype(np.float64)).astype(jnp.bfloat16)
        stacked.append(np.concatenate([high, low], axis=0))
    return wave, np.stack(stacked)


def cell_kernel(u_ref, v_ref, wave_ref, order_ref, cos_ref, sin_ref, hot_ref, *, side):
    lanes = wave_ref.shape[1]
    u = u_ref[...]
    for r in range(0, side // 4, 8):
        row = lax.broadcasted_iota(jnp.int32, (8, lanes), 0) + r
        for c in range(0, u.shape[1], lanes):
            index = row * u[:, c : c + lanes] % side
            cos_ref[r : r + 8, c : c + lanes] = jnp.take_along_axis(wave_ref[0:8, :], index, axis=1)
            sin_ref[r : r + 8, c : c + lanes] = jnp.take_along_axis(wave_ref[8:16, :], index, axis=1)
    code = (u & 3) * (side // 2) + v_ref[...]
    rows = lax.broadcasted_iota(jnp.int32, (2 * side, u.shape[1]), 0)
    hot_ref[...] = jnp.where(rows == code, 1.0, 0.0).T.astype(BF16)


def split(value):
    high = value.astype(BF16)
    return high, (value - high.astype(F32)).astype(BF16)


def image_kernel(slot_ref, cos_ref, sin_ref, hot_ref, last_ref, *refs, side, weight, batch):
    pieces, refs = refs[:-10], refs[-10:]
    image_hbm, snr_ref, real_ref, imag_ref, peak_ref, power_ref, image_ref, sem, lefts, mids = refs
    trials, cells = pieces[0].shape[0], pieces[0].shape[1] // 2
    total = real_ref.shape[2]
    quarter = side // 4
    for b, piece in enumerate(pieces):
        lanes = pl.ds(pl.multiple_of((slot_ref[0] ^ b) * cells, cells), cells)
        value = (piece[...] * weight).reshape(trials // batch, batch, 2 * cells)
        real_ref[:, :, lanes] = value[:, :, :cells]
        imag_ref[:, :, lanes] = value[:, :, cells:]

    def image_copy(step):
        rows = pl.ds(step * batch, batch)
        return pltpu.make_async_copy(image_ref.at[rows], image_hbm.at[rows], sem.at[step])

    def load(step):
        for i in range(batch):
            real, imag = real_ref[step, i : i + 1, :], imag_ref[step, i : i + 1, :]
            cosine, sine = cos_ref[...], sin_ref[...]
            for part, value in enumerate((real * cosine - imag * sine, real * sine + imag * cosine)):
                rows = slice((2 * i + part) * quarter, (2 * i + part + 1) * quarter)
                high, low = split(value)
                lefts[step % 2, rows, :total] = high
                lefts[step % 2, rows, total:] = low

    def gather(step):
        left = lefts.at[step % 2]
        sums = jnp.dot(left[:, :total], hot_ref[...], preferred_element_type=F32)
        sums = sums + jnp.dot(left[:, total:], hot_ref[...], preferred_element_type=F32)
        first, second = sums[:, :side], sums[:, side:]
        for which, value in enumerate((first + second, first - second)):
            value = value.reshape(batch, 2, quarter, side)
            value = jnp.concatenate([value[:, 0], value[:, 1]], axis=2).reshape(batch * quarter, 2 * side)
            high, low = split(value)
            mids[step % 2, which, 0] = high
            mids[step % 2, which, 1] = low

    def turn(step):
        found = []
        for which in range(2):
            high, low = mids[step % 2, which, 0], mids[step % 2, which, 1]
            image = jnp.dot(low, last_ref[which, : 2 * side], preferred_element_type=F32)
            image = image + jnp.dot(high, last_ref[which, 2 * side :], preferred_element_type=F32)
            found.append(image + jnp.dot(high, last_ref[which, : 2 * side], preferred_element_type=F32))
        for i in range(batch):
            peak, power = None, None
            for q in range(4):
                half = slice(side * (q // 2), side * (q // 2 + 1))
                tile = found[q % 2][i * quarter : (i + 1) * quarter, half]
                image_ref[step * batch + i, q * quarter : (q + 1) * quarter, :] = tile
                peak = tile if q == 0 else jnp.maximum(peak, tile)
                power = tile * tile if q == 0 else power + tile * tile
            peak_ref[step, i : i + 1, :] = jnp.max(peak, axis=0, keepdims=True)
            power_ref[step, i : i + 1, :] = jnp.sum(power, axis=0, keepdims=True)
        image_copy(step).start()

    steps = trials // batch
    for step in range(steps + 2):
        if step >= 2:
            turn(step - 2)
        if 1 <= step <= steps:
            gather(step - 1)
        if step < steps:
            load(step)
    peak = jnp.max(peak_ref[...].reshape(trials, side), axis=1, keepdims=True)
    power = jnp.sum(power_ref[...].reshape(trials, side), axis=1, keepdims=True) / (side * side)
    snr = peak / jnp.sqrt(power + 1e-06)
    corner = lax.broadcasted_iota(jnp.int32, (trials, trials), 0) == lax.broadcasted_iota(jnp.int32, (trials, trials), 1)
    snr_ref[...] = jnp.sum(jnp.where(corner, snr, 0.0), axis=0, keepdims=True)
    for step in range(trials // batch):
        image_copy(step).wait()


def cell_tables(coord_u, coord_v, order, side):
    total = coord_u.shape[0]
    wave, _ = wave_tables(side)
    return pl.pallas_call(
        functools.partial(cell_kernel, side=side),
        in_specs=[VMEM] * 3 + [pl.BlockSpec(memory_space=pl.ANY)],
        out_specs=[VMEM] * 3,
        out_shape=[jax.ShapeDtypeStruct((side // 4, total), F32)] * 2 + [jax.ShapeDtypeStruct((total, 2 * side), BF16)],
        compiler_params=pltpu.CompilerParams(vmem_limit_bytes=16 << 20),
        cost_estimate=pl.CostEstimate(flops=10**9, bytes_accessed=1 << 20, transcendentals=0),
        name="cell_tables",
    )(coord_u.reshape(1, total), coord_v.reshape(1, total), jnp.asarray(wave), order)


def picture(pieces, slot, cells, side, weight):
    trials = pieces[0].shape[0]
    total = cells[0].shape[1]
    batch = math.gcd(16, trials)
    _, last = wave_tables(side)
    images, snr = pl.pallas_call(
        functools.partial(image_kernel, side=side, weight=weight, batch=batch),
        in_specs=[pl.BlockSpec(memory_space=pltpu.SMEM)] + [VMEM] * (4 + len(pieces)),
        out_specs=[pl.BlockSpec(memory_space=pltpu.HBM), VMEM],
        out_shape=[jax.ShapeDtypeStruct((trials, side, side), F32), jax.ShapeDtypeStruct((1, trials), F32)],
        scratch_shapes=[pltpu.VMEM((trials // batch, batch, total), F32)] * 2
        + [pltpu.VMEM((trials // batch, batch, side), F32)] * 2
        + [
            pltpu.VMEM((trials, side, side), F32),
            pltpu.SemaphoreType.DMA((trials // batch,)),
            pltpu.VMEM((2, batch * side // 2, 2 * total), BF16),
            pltpu.VMEM((2, 2, 2, batch * side // 4, 2 * side), BF16),
        ],
        compiler_params=pltpu.CompilerParams(vmem_limit_bytes=32 << 20),
        name="picture",
    )(slot.reshape(1), *cells, jnp.asarray(last), *pieces)
    return images, snr.reshape(trials)


def swap(value, axes, size, step):
    return lax.ppermute(value, axes, [(i, i ^ step) for i in range(size)])


def shards(visibilities, flags, delays, coord_u, coord_v, *, sizes):
    channels, times = visibilities.shape[1:3]
    trials, total_channels = delays.shape
    near = sizes["pol"] * sizes["sub"]
    own = trials // sizes["uv"]
    position = lax.axis_index("uv")
    slot = lax.axis_index(("pol", "sub"))
    scale = 1.0 / math.sqrt(total_channels * times)
    weight = 2.0 / math.sqrt(coord_u.shape[0])
    if own % 128 or channels % 128:
        rows = lax.dynamic_slice_in_dim(delays, position * channels, channels, 1)
        part = dedisperse_first(flags, rows, visibilities, scale, 1)[0]
        width = part.shape[1]
        part = part.reshape(sizes["uv"] * near, -1, width)
        held = lax.all_to_all(part, AXES, split_axis=0, concat_axis=0, tiled=True)
        held = held.reshape(sizes["uv"], near, -1, width).sum(axis=0)
        pieces = [lax.dynamic_index_in_dim(held, slot ^ i, 0, keepdims=False) for i in range(near)]
        return picture(pieces, slot, cell_tables(coord_u, coord_v, part, IMG), IMG, weight)

    last = sizes["uv"] - 1
    part, turned, sums, table, *rows = dedisperse_first(flags, delays, visibilities, scale, sizes["uv"])
    held = [swap(part, "uv", sizes["uv"], last)]
    for step in range(last - 1, -1, -1):
        part = dedisperse_next(rows[step], table, turned, sums, part, scale)
        if step:
            held.append(swap(part, "uv", sizes["uv"], step))
    for other in held:
        part = part + other
    cells = cell_tables(coord_u, coord_v, part, IMG)
    part = part.reshape(near, own // near, part.shape[1])
    pieces = [lax.dynamic_index_in_dim(part, slot ^ i, 0, keepdims=False) for i in range(near)]
    for i in range(near - 1, 0, -1):
        pieces[i] = swap(pieces[i], ("pol", "sub"), near, i)
    return picture(pieces, slot, cells, IMG, weight)


def solution(mesh):
    in_specs = (P(None, "uv", "groups", ("pol", "sub")), P(("groups", "uv")), P(), P(), P())
    out_specs = (P(("groups", "uv", "pol", "sub"), None, None), P(("groups", "uv", "pol", "sub")))
    body = functools.partial(shards, sizes=dict(mesh.shape))
    return jax.shard_map(body, mesh=mesh, in_specs=in_specs, out_specs=out_specs, check_vma=False)
```
